128 devices in a mesh: section: 2 (over y_lo), dp: 4 (over x), shard: 16 (over y_hi, z, core).
Axes of the slice: x: 4, y: 4 (y_hi: 2, y_lo: 2; y = y_hi * 2 + y_lo), z: 4, core: 2. Of those that a mesh axis runs over, the one named last changes fastest.
Arguments:
- features: bfloat16 [2, 2048, 6144], P('section', ('dp', 'shard')), may hold values from -6 to 6
- delayed_error: bfloat16 [2, 2048, 6144], P('section', ('dp', 'shard')), may hold values from -6 to 6
- ln_gain: float32 [2, 6144], P('section'), may hold values from 0.25 to 1.75
- w_in: bfloat16 [2, 6144, 12288], P('section', None, 'shard'), may hold values from -0.078125 to 0.078125
- w_out: bfloat16 [2, 12288, 6144], P('section', 'shard'), may hold values from -0.0546875 to 0.0546875
Outputs:
- passed_error: bfloat16 [2, 2048, 6144], P('section', ('dp', 'shard'))
- gain_grad: float32 [2, 6144], P('section')
- w_in_grad: bfloat16 [2, 6144, 12288], P('section', 'dp', 'shard')
- w_out_grad: bfloat16 [2, 12288, 6144], P('section', 'shard', 'dp')
The draws below stay inside these ranges and needn't reach their ends.
All inputs are finite; a program needn't handle non-finite values.
Results may differ from the reference program's by a relative error of at most 0.013.
Values may be sent and summed in bfloat16 or wider, within the bound.
A program may use at most 192 MiB of HBM per device.

```python
import jax
import jax.numpy as jnp
from jax import lax

D = 6144
FF = 12288
TOK_DEV = 32
TOKENS = 2048
SECTIONS = 2
N_SECTION = 2
N_DP = 4
N_SHARD = 16


def shard_levels(key, extent, split, smallest, top_value):
    def one(dim, blocks):
        steps = jax.random.uniform(jax.random.fold_in(jax.random.fold_in(key, 6), dim), (blocks,), jnp.float32, smallest / len(split), top_value / len(split))
        return jnp.repeat(jnp.exp(steps), extent[dim] // blocks).reshape((-1,) + (1,) * (len(extent) - dim - 1))

    loudness = one(*split[0])
    for cut in split[1:]:
        loudness = loudness * one(*cut)
    return loudness


def scatter_about(own_key, shape, deviation, limit, pieces=(), kind=jnp.bfloat16):
    array = jax.random.normal(own_key, shape, jnp.float32) * deviation
    if len(pieces) > 0:
        array = shard_levels(own_key, shape, pieces, -0.22, 0.18) * array
    return jnp.clip(array, min=-limit, max=limit).astype(kind)


def setup_inputs(seed: int = 0) -> dict:
    keys = jax.random.split(jax.random.key(seed), 6)
    features = scatter_about(keys[0], (SECTIONS, TOKENS, D), 1.0, 6.0, ((0, 2), (1, 64)))
    delayed_error = scatter_about(keys[1], (SECTIONS, TOKENS, D), 1.0, 6.0, ((0, 2), (1, 64)))
    ln_gain = jnp.clip(1.0 + 0.15 * jax.random.normal(keys[2], (SECTIONS, D), jnp.float32), 0.25, 1.75)
    w_in = scatter_about(keys[3], (SECTIONS, D, FF), D ** -0.5, 0.078125, ((0, 2), (2, 16)))
    w_out = scatter_about(keys[4], (SECTIONS, FF, D), FF ** -0.5, 0.0546875, ((0, 2), (1, 16)))
    return dict(features=features, delayed_error=delayed_error, ln_gain=ln_gain, w_in=w_in, w_out=w_out)


SQRT_HALF = 0.7071067811865476
INV_ROOT_TWO_PI = 0.3989422804014327
EPSILON = 1e-06

def rounded(values):
    return lax.optimization_barrier(values.astype(jnp.bfloat16)).astype(jnp.float32)

def one_module(features, errors, scale, w_in, w_out):
    values = features.astype(jnp.float32)
    average = lax.optimization_barrier(jnp.mean(values, -1, keepdims=True))
    centred = values - average
    variance = lax.optimization_barrier(jnp.mean(centred * centred, -1, keepdims=True))
    inverse = lax.rsqrt(variance + EPSILON)
    centred = centred * inverse
    normed = (centred * scale).astype(jnp.bfloat16)
    pre = jnp.dot(normed, w_in, preferred_element_type=jnp.float32)
    normal_cdf = 0.5 * (1.0 + jax.scipy.special.erf(pre * SQRT_HALF))
    density = INV_ROOT_TWO_PI * jnp.exp(-0.5 * pre * pre)
    active = (pre * normal_cdf).astype(jnp.bfloat16)
    back_act = jnp.dot(errors, w_out.T, preferred_element_type=jnp.float32)
    pre_error = (back_act * (normal_cdf + pre * density)).astype(jnp.bfloat16)
    width = FF // N_SHARD
    norm_error = jnp.zeros((TOKENS, D), jnp.float32)
    for column_block in range(N_SHARD):
        lower = column_block * width
        term = jnp.dot(pre_error[:, lower:lower + width], w_in[:, lower:lower + width].T, preferred_element_type=jnp.float32)
        norm_error = norm_error + rounded(term)
    scaled = norm_error * scale
    corrected = inverse * (scaled - lax.optimization_barrier(jnp.mean(scaled, -1, keepdims=True)) - centred * lax.optimization_barrier(jnp.mean(scaled * centred, -1, keepdims=True)))
    own_error = (errors.astype(jnp.float32) + corrected).astype(jnp.bfloat16)
    gain_grad = lax.optimization_barrier(jnp.sum(norm_error * centred, 0))
    group = TOK_DEV * N_SHARD
    in_grad = jnp.zeros((D, FF), jnp.float32)
    out_grad = jnp.zeros((FF, D), jnp.float32)
    for group_index in range(N_DP):
        lower = group_index * group
        in_grad = in_grad + rounded(jnp.dot(normed[lower:lower + group].T, pre_error[lower:lower + group], preferred_element_type=jnp.float32))
        out_grad = out_grad + rounded(jnp.dot(active[lower:lower + group].T, errors[lower:lower + group], preferred_element_type=jnp.float32))
    return (own_error, gain_grad, in_grad.astype(jnp.bfloat16), out_grad.astype(jnp.bfloat16))

def reference(features, delayed_error, ln_gain, w_in, w_out):
    results = []
    for section_number in range(N_SECTION):
        results.append(one_module(features[section_number], delayed_error[section_number], ln_gain[section_number], w_in[section_number], w_out[section_number]))
    passed_error = jnp.stack([results[(section_number + 1) % N_SECTION][0] for section_number in range(N_SECTION)])
    gain_grad = jnp.stack([entry[1] for entry in results])
    w_in_grad = jnp.stack([entry[2] for entry in results])
    w_out_grad = jnp.stack([entry[3] for entry in results])
    return (passed_error, gain_grad, w_in_grad, w_out_grad)
```

```python
import functools

import jax
import jax.numpy as jnp
from jax import lax
from jax.experimental import pallas as pl
from jax.experimental.pallas import tpu as pltpu
from jax.sharding import PartitionSpec as P

SQRT_HALF = 0.7071067811865476
INV_ROOT_TWO_PI = 0.3989422804014327
EPSILON = 1e-06
F32 = jnp.float32
BF16 = jnp.bfloat16
MESH = pl.DeviceIdType.MESH
W = 768
TOK = 32
GROUP = 512
PIECES = 8
LIMIT = 66_900_000

Y0, ZP, ZM, YZP, YZM, FA, FB, YFA, YFB = range(9)


def place():
    s = lax.axis_index("section")
    d = lax.axis_index("dp")
    j = lax.axis_index("shard")
    return s, d, j // 8, (j // 2) % 4, j % 2


def neighbour(dx=0, dh=0, dz=0, dc=0):
    s, d, h, z, c = place()
    return (
        s,
        (d + dx + 4) % 4,
        ((h + dh) % 2) * 8 + ((z + dz + 4) % 4) * 2 + (c + dc) % 2,
    )


def greet(barrier, targets):
    for target in targets:
        pl.semaphore_signal(barrier, inc=1, device_id=target, device_id_type=MESH)
    pl.semaphore_wait(barrier, len(targets))


def dot(a, b, ca, cb):
    return lax.dot_general(
        a, b, (((ca,), (cb,)), ((), ())), preferred_element_type=F32
    )


class Gather:
    def __init__(self, bufs, send, recv, core_recv):
        self.bufs, self.send, self.recv, self.core_recv = bufs, send, recv, core_recv

    def rows(self, dh, dz, dc=0, first=0, count=TOK):
        _, _, h, z, c = place()
        block = ((h + dh) % 2) * 8 + ((z + dz + 4) % 4) * 2 + (c + dc) % 2
        return pl.ds(pl.multiple_of(block * TOK + first, 16), count)

    def copy(self, p, a, rows, sem, target, source=None):
        there = self.bufs[a].at[p, rows, :]
        return pltpu.make_async_remote_copy(
            src_ref=there if source is None else source,
            dst_ref=there,
            send_sem=self.send.at[p, a],
            recv_sem=sem,
            device_id=target,
            device_id_type=MESH,
        )

    def put(self, p, a, rows, kind, target, source=None):
        self.copy(p, a, rows, self.recv.at[p, a, kind], target, source).start()

    def got(self, p, a, rows, kind):
        self.copy(p, a, rows, self.recv.at[p, a, kind], neighbour(dz=1)).wait_recv()

    def to_core(self, p, a, dh, dz, source=None):
        rows = self.rows(dh, dz)
        sem = self.core_recv.at[p, a, dh * 4 + dz % 4]
        self.copy(p, a, rows, sem, neighbour(dc=1), source).start()

    def stage0(self, p, sources):
        up, down, across = neighbour(dz=1), neighbour(dz=-1), neighbour(dh=1)
        own = self.rows(0, 0)
        for a in range(2):
            self.put(p, a, own, Y0, across, sources[a])
            self.put(p, a, own, ZM, up, sources[a])
            self.put(p, a, own, ZP, down, sources[a])
            self.to_core(p, a, 0, 0, sources[a])

    def stage1(self, p):
        up, down, across = neighbour(dz=1), neighbour(dz=-1), neighbour(dh=1)
        self.got(p, 0, self.rows(1, 0), Y0)
        self.put(p, 0, self.rows(1, 0), YZM, up)
        self.put(p, 0, self.rows(1, 0), YZP, down)
        self.to_core(p, 0, 1, 0)
        for a in range(2):
            self.got(p, a, self.rows(0, 1), ZP)
            self.put(p, a, self.rows(0, 1, 0, 0, 16), FA, down)
            self.to_core(p, a, 0, 1)
            self.got(p, a, self.rows(0, -1), ZM)
            self.put(p, a, self.rows(0, -1, 0, 16, 16), FB, up)
            self.to_core(p, a, 0, -1)
        self.put(p, 1, self.rows(0, 1), YZP, across)
        self.put(p, 1, self.rows(0, -1), YZM, across)
        self.got(p, 1, self.rows(1, 0), Y0)
        self.to_core(p, 1, 1, 0)

    def stage2(self, p):
        up, down, across = neighbour(dz=1), neighbour(dz=-1), neighbour(dh=1)
        self.got(p, 0, self.rows(1, 1), YZP)
        self.put(p, 0, self.rows(1, 1, 0, 0, 16), YFA, down)
        self.to_core(p, 0, 1, 1)
        self.got(p, 0, self.rows(1, -1), YZM)
        self.put(p, 0, self.rows(1, -1, 0, 16, 16), YFB, up)
        self.to_core(p, 0, 1, -1)
        for a in (1, 0):
            self.got(p, a, self.rows(0, 2, 0, 0, 16), FA)
            self.got(p, a, self.rows(0, 2, 0, 16, 16), FB)
            if a == 1:
                self.put(p, 1, self.rows(0, 2), YFA, across)
            self.to_core(p, a, 0, 2)
        self.got(p, 1, self.rows(1, 1), YZP)
        self.to_core(p, 1, 1, 1)
        self.got(p, 1, self.rows(1, -1), YZM)
        self.to_core(p, 1, 1, -1)

    def stage3(self, p):
        self.got(p, 0, self.rows(1, 2, 0, 0, 16), YFA)
        self.got(p, 0, self.rows(1, 2, 0, 16, 16), YFB)
        self.to_core(p, 0, 1, 2)
        self.got(p, 1, self.rows(1, 2), YFA)
        self.to_core(p, 1, 1, 2)

    def stage4(self, p):
        for a in range(2):
            for dh in range(2):
                for dz in range(4):
                    rows = self.rows(dh, dz, 1)
                    sem = self.core_recv.at[p, a, dh * 4 + dz]
                    self.copy(p, a, rows, sem, neighbour(dc=1)).wait_recv()

    def finish(self, p):
        for a in range(2):
            part = self.bufs[a].at[p, pl.ds(0, 480), :]
            pltpu.make_async_copy(part, part, self.send.at[p, a]).wait()


def gather_scratch(pieces):
    return [
        pltpu.SemaphoreType.DMA((pieces, 2)),
        pltpu.SemaphoreType.DMA((pieces, 2, 9)),
        pltpu.SemaphoreType.DMA((pieces, 2, 8)),
    ]


def forward_kernel(
    normed, errors, w_in, w_out,
    pre_error, active, own_normed, own_errors, slice_normed, slice_errors,
    all_normed, all_errors, win, wout, pre, back,
    send, recv, core_recv, x_send, x_recv, w_sem, own_sem,
):
    _, d, _, _, _ = place()
    weights = []
    for p in range(PIECES):
        cols = pl.ds(p * W, W)
        weights.append(
            (
                pltpu.make_async_copy(w_in.at[cols, :], win.at[p], w_sem.at[p, 0]),
                pltpu.make_async_copy(w_out.at[:, cols], wout.at[p], w_sem.at[p, 1]),
            )
        )
        for copy in weights[-1]:
            copy.start()
    gather = Gather((all_normed, all_errors), send, recv, core_recv)
    greet(
        pltpu.get_barrier_semaphore(),
        [neighbour(dx=1), neighbour(dx=-1), neighbour(dx=2), neighbour(dh=1)]
        + [neighbour(dz=1), neighbour(dz=-1), neighbour(dc=1)],
    )
    crossings = []
    for g, dx in enumerate((-1, 1, 2)):
        for half in range(2):
            cols = pl.ds(pl.multiple_of((((d + dx + 4) % 4) * 2 + half) * W, W), W)
            for a, (source, out) in enumerate(
                ((normed, slice_normed), (errors, slice_errors))
            ):
                copy = pltpu.make_async_remote_copy(
                    src_ref=source.at[:, cols],
                    dst_ref=out.at[g * 2 + half],
                    send_sem=x_send.at[g, half, a],
                    recv_sem=x_recv.at[g, half, a],
                    device_id=neighbour(dx=dx),
                    device_id_type=MESH,
                )
                copy.start()
                crossings.append(copy)
    pre[...] = jnp.zeros_like(pre)
    back[...] = jnp.zeros_like(back)

    @pl.loop(0, PIECES + 4)
    def _(t):
        @pl.when(t < PIECES)
        def _():
            cols = pl.ds(pl.multiple_of(t * W, W), W)
            gather.stage0(t, (normed.at[:, cols], errors.at[:, cols]))
            own = gather.rows(0, 0)
            all_normed[t, own, :] = normed[:, cols]
            all_errors[t, own, :] = errors[:, cols]

        @pl.when((t >= 1) & (t < PIECES + 1))
        def _():
            gather.stage1(t - 1)

        @pl.when((t >= 2) & (t < PIECES + 2))
        def _():
            gather.stage2(t - 2)

        @pl.when((t >= 3) & (t < PIECES + 3))
        def _():
            gather.stage3(t - 3)

        @pl.when(t >= 4)
        def _():
            p = t - 4
            gather.stage4(p)
            cols = pl.ds(pl.multiple_of(p * W, W), W)
            pltpu.make_async_copy(w_in.at[cols, :], win.at[p], w_sem.at[p, 0]).wait()
            pltpu.make_async_copy(w_out.at[:, cols], wout.at[p], w_sem.at[p, 1]).wait()
            pre[...] += dot(all_normed[p], win[p], 1, 0)
            back[...] += dot(all_errors[p], wout[p], 1, 1)

    own_copies = []
    for half in range(2):
        for a, (source, out) in enumerate(
            ((all_normed, own_normed), (all_errors, own_errors))
        ):
            copy = pltpu.make_async_copy(
                source.at[d * 2 + half], out.at[half], own_sem.at[half, a]
            )
            copy.start()
            own_copies.append(copy)

    @pl.loop(0, GROUP // 32)
    def _(i):
        rows = pl.ds(pl.multiple_of(i * 32, 32), 32)
        x = pre[rows, :]
        cdf = 0.5 * (1.0 + lax.erf(x * SQRT_HALF))
        density = INV_ROOT_TWO_PI * jnp.exp(-0.5 * x * x)
        active[rows, :] = (x * cdf).astype(BF16)
        pre_error[rows, :] = (back[rows, :] * (cdf + x * density)).astype(BF16)

    for copy in own_copies:
        copy.wait()
    for copy in crossings:
        copy.wait()

    @pl.loop(0, PIECES)
    def _(p):
        gather.finish(p)


def backward_kernel(
    pre_error, active, own_normed, own_errors, slice_normed, slice_errors, w_in,
    norm_error, in_grad, out_grad,
    all_normed, all_errors, acts, win, part, paired, summed, hop1, hop2, total, last,
    in_acc, out_acc,
    send, recv, core_recv, x_send, x_recv, f_send, f_recv, w_sem, own_sem,
    rs_send, rs_recv,
):
    _, _, h, z, c = place()
    gather = Gather((all_normed, all_errors), send, recv, core_recv)
    loads = []
    for half in range(2):
        for a, (source, buf) in enumerate(
            ((own_normed, all_normed), (own_errors, all_errors))
        ):
            loads.append(
                pltpu.make_async_copy(
                    source.at[half], buf.at[6 + half], own_sem.at[half, a]
                )
            )
    for copy in loads:
        copy.start()

    def weight(q):
        cols = pl.ds(pl.multiple_of(q * W, W), W)
        return pltpu.make_async_copy(w_in.at[cols, :], win.at[q], w_sem.at[q])

    for q in range(PIECES):
        weight(q).start()
    mine = (pre_error, active)
    up, down, left, right = (
        neighbour(dz=1), neighbour(dz=-1), neighbour(dx=-1), neighbour(dx=1),
    )
    across, other = neighbour(dh=1), neighbour(dc=1)
    greet(
        pltpu.get_barrier_semaphore(), [up, down, left, right, across, other]
    )
    low, high = pl.ds(0, 256), pl.ds(256, 256)

    def sideways(a, g, half):
        rows = pl.ds(half * 256, 256)
        return pltpu.make_async_remote_copy(
            src_ref=mine[a].at[rows, :],
            dst_ref=acts.at[a, g, rows, :],
            send_sem=x_send.at[a, g, half],
            recv_sem=x_recv.at[a, g, half],
            device_id=(left, right)[g],
            device_id_type=MESH,
        )

    def onward(a, g):
        rows = (low, high)[g]
        return pltpu.make_async_remote_copy(
            src_ref=acts.at[a, g, rows, :],
            dst_ref=acts.at[a, 2, rows, :],
            send_sem=f_send.at[a, g],
            recv_sem=f_recv.at[a, g],
            device_id=(left, right)[g],
            device_id_type=MESH,
        )

    for first in range(2):
        for a in range(2):
            for g in range(2):
                sideways(a, g, g if first == 0 else 1 - g).start()

    for a in range(2):
        acts[a, 3] = mine[a][...]
    in_acc[...] = jnp.zeros_like(in_acc)
    out_acc[...] = jnp.zeros_like(out_acc)

    def move(k, q, source, target_ref, target):
        return pltpu.make_async_remote_copy(
            src_ref=source,
            dst_ref=target_ref,
            send_sem=rs_send.at[q, k],
            recv_sem=rs_recv.at[q, k],
            device_id=target,
            device_id_type=MESH,
        )

    zp, zm, zz = (z + 1) % 4, (z + 3) % 4, (z + 2) % 4
    first16, last16 = pl.ds(0, 16), pl.ds(16, 16)

    def moves(q):
        return (
            move(0, q, part.at[q, :, :, 1 - c], paired.at[q], other),
            move(1, q, summed.at[q, :, zz, first16, :], hop1.at[q, 0], up),
            move(2, q, summed.at[q, :, zz, last16, :], hop1.at[q, 1], down),
            move(3, q, summed.at[q, :, zp], hop2.at[q, 0], up),
            move(4, q, summed.at[q, :, zm], hop2.at[q, 1], down),
            move(5, q, total.at[q, 1 - h], last.at[q], across),
        )

    def scatter0(q):
        weight(q).wait()
        value = dot(pre_error[...], win[q], 1, 1).astype(BF16)
        part[q] = value.reshape(2, 4, 2, TOK, W)
        moves(q)[0].start()

    def scatter1(q):
        m = moves(q)
        m[0].wait_recv()
        for hh in range(2):
            for zi in range(4):
                summed[q, hh, zi] = (
                    part[q, hh, zi, c].astype(F32) + paired[q, hh, zi].astype(F32)
                ).astype(BF16)
        m[1].start()
        m[2].start()

    def scatter2(q):
        m = moves(q)
        for k, row, rows in ((0, zp, first16), (1, zm, last16)):
            m[1 + k].wait_recv()
            for hh in range(2):
                summed[q, hh, row, rows, :] = (
                    summed[q, hh, row, rows, :].astype(F32)
                    + hop1[q, k, hh].astype(F32)
                ).astype(BF16)
            m[3 + k].start()

    def scatter3(q):
        m = moves(q)
        m[3].wait_recv()
        m[4].wait_recv()
        for hh in range(2):
            total[q, hh] = (
                summed[q, hh, z].astype(F32)
                + hop2[q, 0, hh].astype(F32)
                + hop2[q, 1, hh].astype(F32)
            ).astype(BF16)
        m[5].start()

    def scatter4(q):
        moves(q)[5].wait_recv()
        cols = pl.ds(pl.multiple_of(q * W, W), W)
        norm_error[:, cols] = total[q, h].astype(F32) + last[q].astype(F32)

    def unit(u, g, half):
        in_acc[half] += dot(all_normed[u], acts[0, g], 0, 0)
        out_acc[half] += dot(acts[1, g], all_errors[u], 0, 0)

    @pl.loop(0, PIECES + 4)
    def _(t):
        @pl.when(t < PIECES)
        def _():
            scatter0(t)

        @pl.when(t < 6)
        def _():
            gather.stage0(t, (slice_normed.at[t], slice_errors.at[t]))
            own = gather.rows(0, 0)
            all_normed[t, own, :] = slice_normed[t]
            all_errors[t, own, :] = slice_errors[t]

        @pl.when((t >= 1) & (t < PIECES + 1))
        def _():
            scatter1(t - 1)

        @pl.when((t >= 2) & (t < PIECES + 2))
        def _():
            scatter2(t - 2)

        @pl.when((t >= 1) & (t < 7))
        def _():
            gather.stage1(t - 1)

        @pl.when((t >= 3) & (t < PIECES + 3))
        def _():
            scatter3(t - 3)

        @pl.when((t >= 2) & (t < 8))
        def _():
            gather.stage2(t - 2)

        @pl.when(t >= 4)
        def _():
            scatter4(t - 4)

        @pl.when((t >= 3) & (t < 9))
        def _():
            gather.stage3(t - 3)

        @pl.when(t == 1)
        def _():
            for copy in loads:
                copy.wait()

        @pl.when(t == 5)
        def _():
            for a in range(2):
                for g in range(2):
                    sideways(a, g, g).wait_recv()
                    onward(a, g).start()

        @pl.when(t == 8)
        def _():
            for a in range(2):
                for g in range(2):
                    sideways(a, g, 1 - g).wait_recv()

        @pl.when(t == PIECES + 3)
        def _():
            for a in range(2):
                for g in range(2):
                    onward(a, g).wait_recv()

        @pl.when((t == 1) | (t == 2))
        def _():
            unit(t + 5, 3, t - 1)

        @pl.when(t >= 8)
        def _():
            gather.stage4(t - 8)
            unit(t - 8, (t - 8) // 2, (t - 8) % 2)

    for u in range(4, 6):
        gather.stage4(u)

    @pl.loop(4, 6)
    def _(u):
        unit(u, u // 2, u % 2)

    for half in range(2):
        in_grad[pl.ds(half * W, W), :] = in_acc[half].astype(BF16)
        out_grad[:, pl.ds(half * W, W)] = out_acc[half].astype(BF16)

    for a in range(2):
        for g in range(2):
            sideways(a, g, 0).wait_send()
            sideways(a, g, 1).wait_send()
            onward(a, g).wait_send()

    @pl.loop(0, 6)
    def _(p):
        gather.finish(p)

    @pl.loop(0, PIECES)
    def _(q):
        for m in moves(q):
            m.wait_send()


def shape(dims, dtype=BF16):
    return jax.ShapeDtypeStruct(dims, dtype)


VM = pl.BlockSpec(memory_space=pltpu.VMEM)
ANY = pl.BlockSpec(memory_space=pl.ANY)
DMA = pltpu.SemaphoreType.DMA


def forward_call(normed, errors, w_in, w_out):
    return pl.pallas_call(
        forward_kernel,
        name="forward",
        out_shape=(
            shape((GROUP, W)), shape((GROUP, W)),
            shape((2, GROUP, W)), shape((2, GROUP, W)),
            shape((6, TOK, W)), shape((6, TOK, W)),
        ),
        in_specs=[VM, VM, ANY, ANY],
        out_specs=(VM, VM, ANY, ANY, ANY, ANY),
        scratch_shapes=[
            pltpu.VMEM((PIECES, GROUP, W), BF16),
            pltpu.VMEM((PIECES, GROUP, W), BF16),
            pltpu.VMEM((PIECES, W, W), BF16),
            pltpu.VMEM((PIECES, W, W), BF16),
            pltpu.VMEM((GROUP, W), F32),
            pltpu.VMEM((GROUP, W), F32),
            *gather_scratch(PIECES),
            DMA((3, 2, 2)), DMA((3, 2, 2)), DMA((PIECES, 2)), DMA((2, 2)),
        ],
        compiler_params=pltpu.CompilerParams(
            collective_id=0, has_side_effects=True, vmem_limit_bytes=LIMIT
        ),
    )(normed, errors, w_in, w_out)


def backward_call(*args):
    return pl.pallas_call(
        backward_kernel,
        name="backward",
        out_shape=(
            shape((TOK, W * PIECES), F32), shape((2 * W, W)), shape((W, 2 * W)),
        ),
        in_specs=[VM, VM, ANY, ANY, VM, VM, ANY],
        out_specs=(VM, VM, VM),
        scratch_shapes=[
            pltpu.VMEM((8, GROUP, W), BF16),
            pltpu.VMEM((8, GROUP, W), BF16),
            pltpu.VMEM((2, 4, GROUP, W), BF16),
            pltpu.VMEM((PIECES, W, W), BF16),
            pltpu.VMEM((PIECES, 2, 4, 2, TOK, W), BF16),
            pltpu.VMEM((PIECES, 2, 4, TOK, W), BF16),
            pltpu.VMEM((PIECES, 2, 4, TOK, W), BF16),
            pltpu.VMEM((PIECES, 2, 2, 16, W), BF16),
            pltpu.VMEM((PIECES, 2, 2, TOK, W), BF16),
            pltpu.VMEM((PIECES, 2, TOK, W), BF16),
            pltpu.VMEM((PIECES, TOK, W), BF16),
            pltpu.VMEM((2, W, W), F32),
            pltpu.VMEM((2, W, W), F32),
            *gather_scratch(6),
            DMA((2, 2, 2)), DMA((2, 2, 2)), DMA((2, 2)), DMA((2, 2)),
            DMA((PIECES,)), DMA((2, 2)), DMA((PIECES, 6)), DMA((PIECES, 6)),
        ],
        compiler_params=pltpu.CompilerParams(
            collective_id=1, has_side_effects=True, vmem_limit_bytes=LIMIT
        ),
    )(*args)


def shifted(block, axis, distance):
    devices = range(lax.axis_size(axis))
    route = [((i - distance) % len(devices), i) for i in devices]
    return lax.ppermute(block, axis, route)


def per_device(features, delayed_error, ln_gain, w_in, w_out):
    errors = delayed_error[0]
    scale = ln_gain[0]
    in_block, out_block = w_in[0], w_out[0]
    values = features[0].astype(F32)
    average = jnp.mean(values, -1, keepdims=True)
    centred = values - average
    variance = jnp.mean(centred * centred, -1, keepdims=True)
    inverse = lax.rsqrt(variance + EPSILON)
    centred = centred * inverse
    normed = (centred * scale).astype(BF16)
    pre_error, active, own_n, own_e, slice_n, slice_e = forward_call(
        normed, errors, in_block, out_block
    )
    norm_error, in_total, out_total = backward_call(
        pre_error, active, own_n, own_e, slice_n, slice_e, in_block
    )
    scaled = norm_error * scale
    corrected = inverse * (
        scaled
        - jnp.mean(scaled, -1, keepdims=True)
        - centred * jnp.mean(scaled * centred, -1, keepdims=True)
    )
    own_error = (errors.astype(F32) + corrected).astype(BF16)
    gain_part = jnp.sum(norm_error * centred, 0)
    gain_grad = jnp.sum(lax.all_gather(gain_part, ("dp", "shard")), 0)
    passed = shifted(own_error, "section", -1)
    return passed[None], gain_grad[None], in_total[None], out_total[None]


def solution(mesh):
    return jax.shard_map(
        per_device,
        mesh=mesh,
        in_specs=(
            P("section", ("dp", "shard"), None),
            P("section", ("dp", "shard"), None),
            P("section", None),
            P("section", None, "shard"),
            P("section", "shard", None),
        ),
        out_specs=(
            P("section", ("dp", "shard"), None),
            P("section", None),
            P("section", "dp", "shard"),
            P("section", "shard", "dp"),
        ),
        check_vma=False,
    )
```

```python
import functools

import jax
import jax.numpy as jnp
from jax import lax
from jax.experimental import pallas as pl
from jax.experimental.pallas import tpu as pltpu
from jax.sharding import PartitionSpec as P

SQRT_HALF = 0.7071067811865476
INV_ROOT_TWO_PI = 0.3989422804014327
EPSILON = 1e-06
F32 = jnp.float32
BF16 = jnp.bfloat16
MESH = pl.DeviceIdType.MESH
W = 768
TOK = 32
GROUP = 512
PIECES = 8
ALL = 14
LIMIT = 66_900_000

Y0, ZP, ZM, YZP, YZM, FA, FB, YFA, YFB = range(9)


def place():
    s = lax.axis_index("section")
    d = lax.axis_index("dp")
    j = lax.axis_index("shard")
    return s, d, j // 8, (j // 2) % 4, j % 2


def neighbour(dx=0, dh=0, dz=0, dc=0, ds=0):
    s, d, h, z, c = place()
    return (
        (s + ds) % 2,
        (d + dx + 4) % 4,
        ((h + dh) % 2) * 8 + ((z + dz + 4) % 4) * 2 + (c + dc) % 2,
    )


def greet(barrier, targets):
    for target in targets:
        pl.semaphore_signal(barrier, inc=1, device_id=target, device_id_type=MESH)
    pl.semaphore_wait(barrier, len(targets))


def dot(a, b, ca, cb):
    return lax.dot_general(
        a, b, (((ca,), (cb,)), ((), ())), preferred_element_type=F32
    )


class Gather:
    def __init__(self, bufs, send, recv, core_recv):
        self.bufs, self.send, self.recv, self.core_recv = bufs, send, recv, core_recv

    def rows(self, dh, dz, dc=0, first=0, count=TOK):
        _, _, h, z, c = place()
        block = ((h + dh) % 2) * 8 + ((z + dz + 4) % 4) * 2 + (c + dc) % 2
        return pl.ds(pl.multiple_of(block * TOK + first, 16), count)

    def copy(self, p, a, rows, sem, target, source=None):
        there = self.bufs[a].at[p, rows, :]
        return pltpu.make_async_remote_copy(
            src_ref=there if source is None else source,
            dst_ref=there,
            send_sem=self.send.at[p, a],
            recv_sem=sem,
            device_id=target,
            device_id_type=MESH,
        )

    def put(self, p, a, rows, kind, target, source=None):
        self.copy(p, a, rows, self.recv.at[p, a, kind], target, source).start()

    def got(self, p, a, rows, kind):
        self.copy(p, a, rows, self.recv.at[p, a, kind], neighbour(dz=1)).wait_recv()

    def to_core(self, p, a, dh, dz, source=None):
        rows = self.rows(dh, dz)
        sem = self.core_recv.at[p, a, dh * 4 + dz % 4]
        self.copy(p, a, rows, sem, neighbour(dc=1), source).start()

    def stage0(self, p, sources):
        up, down, across = neighbour(dz=1), neighbour(dz=-1), neighbour(dh=1)
        own = self.rows(0, 0)
        for a in range(2):
            self.put(p, a, own, Y0, across, sources[a])
            self.put(p, a, own, ZM, up, sources[a])
            self.put(p, a, own, ZP, down, sources[a])
            self.to_core(p, a, 0, 0, sources[a])

    def stage1(self, p):
        up, down, across = neighbour(dz=1), neighbour(dz=-1), neighbour(dh=1)
        self.got(p, 0, self.rows(1, 0), Y0)
        self.put(p, 0, self.rows(1, 0), YZM, up)
        self.put(p, 0, self.rows(1, 0), YZP, down)
        self.to_core(p, 0, 1, 0)
        for a in range(2):
            self.got(p, a, self.rows(0, 1), ZP)
            self.put(p, a, self.rows(0, 1, 0, 0, 16), FA, down)
            self.to_core(p, a, 0, 1)
            self.got(p, a, self.rows(0, -1), ZM)
            self.put(p, a, self.rows(0, -1, 0, 16, 16), FB, up)
            self.to_core(p, a, 0, -1)
        self.put(p, 1, self.rows(0, 1), YZP, across)
        self.put(p, 1, self.rows(0, -1), YZM, across)
        self.got(p, 1, self.rows(1, 0), Y0)
        self.to_core(p, 1, 1, 0)

    def stage2(self, p):
        up, down, across = neighbour(dz=1), neighbour(dz=-1), neighbour(dh=1)
        self.got(p, 0, self.rows(1, 1), YZP)
        self.put(p, 0, self.rows(1, 1, 0, 0, 16), YFA, down)
        self.to_core(p, 0, 1, 1)
        self.got(p, 0, self.rows(1, -1), YZM)
        self.put(p, 0, self.rows(1, -1, 0, 16, 16), YFB, up)
        self.to_core(p, 0, 1, -1)
        for a in (1, 0):
            self.got(p, a, self.rows(0, 2, 0, 0, 16), FA)
            self.got(p, a, self.rows(0, 2, 0, 16, 16), FB)
            if a == 1:
                self.put(p, 1, self.rows(0, 2), YFA, across)
            self.to_core(p, a, 0, 2)
        self.got(p, 1, self.rows(1, 1), YZP)
        self.to_core(p, 1, 1, 1)
        self.got(p, 1, self.rows(1, -1), YZM)
        self.to_core(p, 1, 1, -1)

    def stage3(self, p):
        self.got(p, 0, self.rows(1, 2, 0, 0, 16), YFA)
        self.got(p, 0, self.rows(1, 2, 0, 16, 16), YFB)
        self.to_core(p, 0, 1, 2)
        self.got(p, 1, self.rows(1, 2), YFA)
        self.to_core(p, 1, 1, 2)

    def stage4(self, p):
        for a in range(2):
            for dh in range(2):
                for dz in range(4):
                    rows = self.rows(dh, dz, 1)
                    sem = self.core_recv.at[p, a, dh * 4 + dz]
                    self.copy(p, a, rows, sem, neighbour(dc=1)).wait_recv()

    def finish(self, p):
        for a in range(2):
            part = self.bufs[a].at[p, pl.ds(0, 480), :]
            pltpu.make_async_copy(part, part, self.send.at[p, a]).wait()


def gather_scratch(pieces):
    return [
        pltpu.SemaphoreType.DMA((pieces, 2)),
        pltpu.SemaphoreType.DMA((pieces, 2, 9)),
        pltpu.SemaphoreType.DMA((pieces, 2, 8)),
    ]


def kernel(
    features, errors, gain, w_in, w_out,
    passed, gain_grad, in_grad, out_grad,
    all_normed, all_errors, acts, win, wout, part, paired, summed, hop1, hop2, total,
    last, in_acc, out_acc, staged, normed, centred, inverses, norm_error, own_error,
    slice_normed, slice_errors, gains,
    send, recv, core_recv, c_send, c_recv, x_send, x_recv, f_send, f_recv, w_sem,
    o_sem, rs_send, rs_recv, g_send, g_recv, p_send, p_recv,
):
    _, d, h, z, c = place()
    up, down, left, right = (
        neighbour(dz=1), neighbour(dz=-1), neighbour(dx=-1), neighbour(dx=1),
    )
    across, other, partner = neighbour(dh=1), neighbour(dc=1), neighbour(ds=1)

    def load_in(k):
        cols = pl.ds(pl.multiple_of(k % PIECES * W, W), W)
        return pltpu.make_async_copy(
            w_in.at[cols, :], win.at[k % 3], w_sem.at[0, k % 3]
        )

    def load_out(k):
        cols = pl.ds(pl.multiple_of(k * W, W), W)
        return pltpu.make_async_copy(
            w_out.at[:, cols], wout.at[k % 2], w_sem.at[1, k % 2]
        )

    for k in range(3):
        load_in(k).start()
    for k in range(2):
        load_out(k).start()

    scale = gain[...]
    for first in range(0, TOK, 16):
        rows = pl.ds(first, 16)
        values = features[rows, :].astype(F32)
        average = jnp.mean(values, -1, keepdims=True)
        values = values - average
        variance = jnp.mean(values * values, -1, keepdims=True)
        inverse = lax.rsqrt(variance + EPSILON)
        values = values * inverse
        centred[rows, :] = values
        inverses[rows, :] = jnp.broadcast_to(inverse, (16, 128))
        normed[rows, :] = (values * scale).astype(BF16)

    gather = Gather((all_normed, all_errors), send, recv, core_recv)
    greet(
        pltpu.get_barrier_semaphore(),
        [up, down, left, right, across, other, partner]
        + [neighbour(dz=2), neighbour(dx=2), neighbour(dh=1, dc=1)],
    )

    def crossing(g, half, a):
        dx = (-1, 1, 2)[g]
        cols = pl.ds(pl.multiple_of((((d + dx + 4) % 4) * 2 + half) * W, W), W)
        return pltpu.make_async_remote_copy(
            src_ref=(normed, errors)[a].at[:, cols],
            dst_ref=(slice_normed, slice_errors)[a].at[g * 2 + half],
            send_sem=c_send.at[g * 2 + half, a],
            recv_sem=c_recv.at[g * 2 + half, a],
            device_id=neighbour(dx=dx),
            device_id_type=MESH,
        )

    def stage0(p):
        cols = pl.ds(pl.multiple_of(p * W, W), W)
        gather.stage0(p, (normed.at[:, cols], errors.at[:, cols]))
        own = gather.rows(0, 0)
        all_normed[p, own, :] = normed[:, cols]
        all_errors[p, own, :] = errors[:, cols]

    def stage0_slice(p):
        u = p - PIECES
        for a, buf in enumerate((slice_normed, slice_errors)):
            pltpu.make_async_remote_copy(
                src_ref=buf.at[u],
                dst_ref=buf.at[u],
                send_sem=c_send.at[u, a],
                recv_sem=c_recv.at[u, a],
                device_id=right,
                device_id_type=MESH,
            ).wait_recv()
        gather.stage0(p, (slice_normed.at[u], slice_errors.at[u]))
        own = gather.rows(0, 0)
        all_normed[p, own, :] = slice_normed[u]
        all_errors[p, own, :] = slice_errors[u]

    @pl.loop(0, 12)
    def _(t):
        @pl.when(t < PIECES)
        def _():
            stage0(t)

        @pl.when(t == 0)
        def _():
            for g in range(3):
                for half in range(2):
                    for a in range(2):
                        crossing(g, half, a).start()

        @pl.when((t >= 1))
        def _():
            gather.stage1(t - 1)

        @pl.when((t >= 2))
        def _():
            gather.stage2(t - 2)

        @pl.when((t >= 3))
        def _():
            gather.stage3(t - 3)

        @pl.when(t >= PIECES)
        def _():
            stage0_slice(t)

        @pl.when(t >= 4)
        def _():
            p = t - 4
            gather.stage4(p)
            load_in(p).wait()
            load_out(p).wait()
            pre = dot(all_normed[p], win[p % 3], 1, 0)
            back = dot(all_errors[p], wout[p % 2], 1, 1)
            rows = pl.ds(0, GROUP)

            @pl.when(p == 0)
            def _():
                in_acc[0, rows, :] = pre
                in_acc[1, rows, :] = back

            @pl.when(p > 0)
            def _():
                in_acc[0, rows, :] += pre
                in_acc[1, rows, :] += back

            load_in(p + 3).start()

            @pl.when(p < PIECES - 2)
            def _():
                load_out(p + 2).start()

    @pl.loop(0, GROUP // 32)
    def _(i):
        rows = pl.ds(pl.multiple_of(i * 32, 32), 32)
        x = in_acc[0, rows, :]
        cdf = 0.5 * (1.0 + lax.erf(x * SQRT_HALF))
        density = INV_ROOT_TWO_PI * jnp.exp(-0.5 * x * x)
        acts[1, 3, rows, :] = (x * cdf).astype(BF16)
        acts[0, 3, rows, :] = (in_acc[1, rows, :] * (cdf + x * density)).astype(BF16)

    low, high = pl.ds(0, 256), pl.ds(256, 256)

    def sideways(a, g, half):
        rows = (low, high)[half]
        return pltpu.make_async_remote_copy(
            src_ref=acts.at[a, 3, rows, :],
            dst_ref=acts.at[a, g, rows, :],
            send_sem=x_send.at[a, g, half],
            recv_sem=x_recv.at[a, g, half],
            device_id=(left, right)[g],
            device_id_type=MESH,
        )

    def onward(a, g):
        rows = (low, high)[g]
        return pltpu.make_async_remote_copy(
            src_ref=acts.at[a, g, rows, :],
            dst_ref=acts.at[a, 2, rows, :],
            send_sem=f_send.at[a, g],
            recv_sem=f_recv.at[a, g],
            device_id=(left, right)[g],
            device_id_type=MESH,
        )

    for first in range(2):
        for a in range(2):
            for g in range(2):
                sideways(a, g, g if first == 0 else 1 - g).start()

    def move(k, q, source, target_ref, target):
        return pltpu.make_async_remote_copy(
            src_ref=source,
            dst_ref=target_ref,
            send_sem=rs_send.at[q, k],
            recv_sem=rs_recv.at[q, k],
            device_id=target,
            device_id_type=MESH,
        )

    zp, zm, zz = (z + 1) % 4, (z + 3) % 4, (z + 2) % 4
    first16, last16 = pl.ds(0, 16), pl.ds(16, 16)

    def m0(q):
        return move(0, q, part.at[q % 3, :, :, 1 - c], paired.at[q], other)

    def m1(q):
        return move(1, q, summed.at[q, :, zz, first16, :], hop1.at[q, 0], up)

    def m2(q):
        return move(2, q, summed.at[q, :, zz, last16, :], hop1.at[q, 1], down)

    def m3(q):
        return move(3, q, summed.at[q, :, zp], hop2.at[q, 0], up)

    def m4(q):
        return move(4, q, summed.at[q, :, zm], hop2.at[q, 1], down)

    def m5(q):
        return move(5, q, total.at[q, 1 - h], last.at[q], across)

    def scatter0(q):
        @pl.when(q >= 3)
        def _():
            m0(q - 3).wait_send()

        load_in(q + PIECES).wait()
        value = dot(acts[0, 3], win[(q + PIECES) % 3], 1, 1).astype(BF16)
        part[q % 3] = value.reshape(2, 4, 2, TOK, W)
        m0(q).start()

        @pl.when(q < PIECES - 3)
        def _():
            load_in(q + PIECES + 3).start()

    def scatter1(q):
        m0(q).wait_recv()
        for hh in range(2):
            for zi in range(4):
                summed[q, hh, zi] = (
                    part[q % 3, hh, zi, c].astype(F32) + paired[q, hh, zi].astype(F32)
                ).astype(BF16)
        m1(q).start()
        m2(q).start()

    def scatter2(q):
        for k, row, rows, came, go in (
            (0, zp, first16, m1, m3), (1, zm, last16, m2, m4),
        ):
            came(q).wait_recv()
            for hh in range(2):
                summed[q, hh, row, rows, :] = (
                    summed[q, hh, row, rows, :].astype(F32)
                    + hop1[q, k, hh].astype(F32)
                ).astype(BF16)
            go(q).start()

    def scatter3(q):
        m3(q).wait_recv()
        m4(q).wait_recv()
        for hh in range(2):
            total[q, hh] = (
                summed[q, hh, z].astype(F32)
                + hop2[q, 0, hh].astype(F32)
                + hop2[q, 1, hh].astype(F32)
            ).astype(BF16)
        m5(q).start()

    def scatter4(q):
        m5(q).wait_recv()
        cols = pl.ds(pl.multiple_of(q * W, W), W)
        norm_error[:, cols] = total[q, h].astype(F32) + last[q].astype(F32)

    def unit(u, g, half):
        gather.stage4(u)
        in_acc[half] += dot(all_normed[u], acts[0, g], 0, 0)
        out_acc[half] += dot(acts[1, g], all_errors[u], 0, 0)

    @pl.loop(12, PIECES + 16)
    def _(t):
        q = t - 12

        @pl.when(q < PIECES)
        def _():
            scatter0(q)

        @pl.when((q >= 1) & (q < PIECES + 1))
        def _():
            scatter1(q - 1)

        @pl.when((q >= 2) & (q < PIECES + 2))
        def _():
            scatter2(q - 2)

        @pl.when((q >= 3) & (q < PIECES + 3))
        def _():
            scatter3(q - 3)

        @pl.when(q >= 4)
        def _():
            scatter4(q - 4)

        @pl.when(t < ALL)
        def _():
            stage0_slice(t)

        @pl.when(t < ALL + 1)
        def _():
            gather.stage1(t - 1)

        @pl.when(t < ALL + 2)
        def _():
            gather.stage2(t - 2)

        @pl.when(t < ALL + 3)
        def _():
            gather.stage3(t - 3)

        @pl.when((q == 1) | (q == 2))
        def _():
            half = q - 1
            u = d * 2 + half
            in_acc[half] = dot(all_normed[u], acts[0, 3], 0, 0)
            out_acc[half] = dot(acts[1, 3], all_errors[u], 0, 0)

        @pl.when(q == 5)
        def _():
            for a in range(2):
                for g in range(2):
                    sideways(a, g, g).wait_recv()
                    onward(a, g).start()

        @pl.when(q == 8)
        def _():
            for a in range(2):
                for g in range(2):
                    sideways(a, g, 1 - g).wait_recv()

        @pl.when(q >= 8)
        def _():
            unit(q, (q - 8) // 2, q % 2)

    for q in range(PIECES):
        cols = pl.ds(q * W, W)
        product = norm_error[:, cols] * centred[:, cols]
        mine = jnp.sum(product, 0, keepdims=True)
        gains[0, h * 2 + c, pl.ds(q, 1), :] = mine

    def spread(level, k):
        target, slot = (
            ((neighbour(dc=1), neighbour(dh=1), neighbour(dh=1, dc=1))[k], h * 2 + c),
            (neighbour(dz=k + 1), z),
            (neighbour(dx=k + 1), d),
        )[level]
        return pltpu.make_async_remote_copy(
            src_ref=gains.at[level, slot],
            dst_ref=gains.at[level, slot],
            send_sem=g_send.at[level, k],
            recv_sem=g_recv.at[level, k],
            device_id=target,
            device_id_type=MESH,
        )

    def collect(level):
        for k in range(3):
            spread(level, k).wait_recv()
        value = gains[level, 0] + gains[level, 1] + gains[level, 2] + gains[level, 3]
        if level == 2:
            gain_grad[...] = value
            return
        gains[level + 1, (z, d)[level]] = value
        for k in range(3):
            spread(level + 1, k).start()

    for k in range(3):
        spread(0, k).start()

    for first in range(0, TOK, 16):
        rows = pl.ds(first, 16)
        scaled = norm_error[rows, :] * scale
        around = centred[rows, :]
        shift = jnp.mean(scaled, -1, keepdims=True)
        slope = jnp.mean(scaled * around, -1, keepdims=True)
        corrected = inverses[rows, pl.ds(0, 1)] * (scaled - shift - around * slope)
        own_error[rows, :] = (errors[rows, :].astype(F32) + corrected).astype(BF16)
    swap = pltpu.make_async_remote_copy(
        src_ref=own_error,
        dst_ref=passed,
        send_sem=p_send,
        recv_sem=p_recv,
        device_id=partner,
        device_id_type=MESH,
    )
    swap.start()

    for a in range(2):
        for g in range(2):
            onward(a, g).wait_recv()

    def emit(half):
        part_of = pl.ds(pl.multiple_of(half * W, W), W)
        return (
            pltpu.make_async_copy(staged.at[0], in_grad.at[part_of, :], o_sem.at[0]),
            pltpu.make_async_copy(staged.at[1], out_grad.at[:, part_of], o_sem.at[1]),
        )

    @pl.loop(0, 2)
    def _(half):
        unit(12 + half, 2, half)

        @pl.when(half == 1)
        def _():
            for copy in emit(0):
                copy.wait()

        staged[0] = in_acc[half].astype(BF16)
        staged[1] = out_acc[half].astype(BF16)
        for copy in emit(half):
            copy.start()

        @pl.when(half == 0)
        def _():
            collect(0)

        @pl.when(half == 1)
        def _():
            collect(1)

    for g in range(3):
        for half in range(2):
            for a in range(2):
                crossing(g, half, a).wait_send()
    for a in range(2):
        for g in range(2):
            sideways(a, g, 0).wait_send()
            sideways(a, g, 1).wait_send()
            onward(a, g).wait_send()

    @pl.loop(0, ALL)
    def _(p):
        gather.finish(p)

    @pl.loop(0, PIECES)
    def _(q):
        @pl.when(q >= PIECES - 3)
        def _():
            m0(q).wait_send()

        for m in (m1, m2, m3, m4, m5):
            m(q).wait_send()

    collect(2)
    for level in range(3):
        for k in range(3):
            spread(level, k).wait_send()
    swap.wait()
    for copy in emit(1):
        copy.wait()


def shape(dims, dtype=BF16):
    return jax.ShapeDtypeStruct(dims, dtype)


VM = pl.BlockSpec(memory_space=pltpu.VMEM)
ANY = pl.BlockSpec(memory_space=pl.ANY)
DMA = pltpu.SemaphoreType.DMA


def block_call(features, errors, gain, w_in, w_out):
    bf16, f32 = functools.partial(pltpu.VMEM, dtype=BF16), functools.partial(
        pltpu.VMEM, dtype=F32
    )
    return pl.pallas_call(
        kernel,
        name="block",
        out_shape=(
            shape((TOK, W * PIECES)), shape((8, W), F32),
            shape((2 * W, W)), shape((W, 2 * W)),
        ),
        in_specs=[VM, VM, VM, ANY, ANY],
        out_specs=(ANY, VM, ANY, ANY),
        scratch_shapes=[
            bf16((ALL, GROUP, W)),
            bf16((ALL, GROUP, W)),
            bf16((2, 4, GROUP, W)),
            bf16((3, W, W)),
            bf16((2, W, W)),
            bf16((3, 2, 4, 2, TOK, W)),
            bf16((PIECES, 2, 4, TOK, W)),
            bf16((PIECES, 2, 4, TOK, W)),
            bf16((PIECES, 2, 2, 16, W)),
            bf16((PIECES, 2, 2, TOK, W)),
            bf16((PIECES, 2, TOK, W)),
            bf16((PIECES, TOK, W)),
            f32((2, W, W)),
            f32((2, W, W)),
            bf16((2, W, W)),
            bf16((TOK, W * PIECES)),
            f32((TOK, W * PIECES)),
            f32((TOK, 128)),
            f32((TOK, W * PIECES)),
            bf16((TOK, W * PIECES)),
            bf16((6, TOK, W)),
            bf16((6, TOK, W)),
            f32((3, 4, 8, W)),
            *gather_scratch(ALL),
            DMA((6, 2)), DMA((6, 2)), DMA((2, 2, 2)), DMA((2, 2, 2)),
            DMA((2, 2)), DMA((2, 2)), DMA((2, 3)), DMA((2,)),
            DMA((PIECES, 6)), DMA((PIECES, 6)), DMA((3, 3)), DMA((3, 3)),
            DMA, DMA,
        ],
        compiler_params=pltpu.CompilerParams(
            collective_id=0, has_side_effects=True, vmem_limit_bytes=LIMIT
        ),
    )(features, errors, gain, w_in, w_out)


def per_device(features, delayed_error, ln_gain, w_in, w_out):
    passed, gain_grad, in_total, out_total = block_call(
        features[0], delayed_error[0], ln_gain, w_in[0], w_out[0]
    )
    return passed[None], gain_grad.reshape(1, -1), in_total[None], out_total[None]


def solution(mesh):
    return jax.shard_map(
        per_device,
        mesh=mesh,
        in_specs=(
            P("section", ("dp", "shard"), None),
            P("section", ("dp", "shard"), None),
            P("section", None),
            P("section", None, "shard"),
            P("section", "shard", None),
        ),
        out_specs=(
            P("section", ("dp", "shard"), None),
            P("section", None),
            P("section", "dp", "shard"),
            P("section", "shard", "dp"),
        ),
        check_vma=False,
    )
```

```python
import functools

import jax
import jax.numpy as jnp
from jax import lax
from jax.experimental import pallas as pl
from jax.experimental.pallas import tpu as pltpu
from jax.sharding import PartitionSpec as P

SQRT_HALF = 0.7071067811865476
INV_ROOT_TWO_PI = 0.3989422804014327
EPSILON = 1e-06
F32 = jnp.float32
BF16 = jnp.bfloat16
MESH = pl.DeviceIdType.MESH
W = 768
WIDE = 2 * W
HALF = 16
TOK = 32
GROUP = 512
PIECES = 8
ALL = 14
LIMIT = 66_900_000

Y0, ZP, ZM, YZP, YZM, FA, FB, YFA, YFB = range(9)


def place():
    s = lax.axis_index("section")
    d = lax.axis_index("dp")
    j = lax.axis_index("shard")
    return s, d, j // 8, (j // 2) % 4, j % 2


def neighbour(dx=0, dh=0, dz=0, dc=0, ds=0):
    s, d, h, z, c = place()
    return (
        (s + ds) % 2,
        (d + dx + 4) % 4,
        ((h + dh) % 2) * 8 + ((z + dz + 4) % 4) * 2 + (c + dc) % 2,
    )


def greet(barrier, targets):
    for target in targets:
        pl.semaphore_signal(barrier, inc=1, device_id=target, device_id_type=MESH)
    pl.semaphore_wait(barrier, len(targets))


def dot(a, b, ca, cb):
    return lax.dot_general(
        a, b, (((ca,), (cb,)), ((), ())), preferred_element_type=F32
    )


FULL, LEFT, RIGHT = pl.ds(0, WIDE), pl.ds(0, W), pl.ds(W, W)


class Gather:
    def __init__(self, bufs, send, recv, core_recv):
        self.bufs, self.send, self.recv, self.core_recv = bufs, send, recv, core_recv

    def block(self, dh, dz, dc=0):
        _, _, h, z, c = place()
        index = ((h + dh) % 2) * 8 + ((z + dz + 4) % 4) * 2 + (c + dc) % 2
        return pl.ds(pl.multiple_of(index * HALF, HALF), HALF)

    def copy(self, p, a, rows, sem, target, source=None, cols=FULL):
        there = self.bufs[a].at[p, rows, cols]
        return pltpu.make_async_remote_copy(
            src_ref=there if source is None else source,
            dst_ref=there,
            send_sem=self.send.at[p, a],
            recv_sem=sem,
            device_id=target,
            device_id_type=MESH,
        )

    def put(self, p, a, rows, kind, target, source=None, cols=FULL):
        sem = self.recv.at[p, a, kind]
        self.copy(p, a, rows, sem, target, source, cols).start()

    def got(self, p, a, rows, kind, cols=FULL):
        sem = self.recv.at[p, a, kind]
        self.copy(p, a, rows, sem, neighbour(dz=1), None, cols).wait_recv()

    def to_core(self, p, a, dh, dz, source=None):
        sem = self.core_recv.at[p, a, dh * 4 + dz % 4]
        self.copy(p, a, self.block(dh, dz), sem, neighbour(dc=1), source).start()

    def stage0(self, p, sources):
        up, down, across = neighbour(dz=1), neighbour(dz=-1), neighbour(dh=1)
        own = self.block(0, 0)
        for a in range(2):
            self.put(p, a, own, Y0, across, sources[a])
            self.put(p, a, own, ZM, up, sources[a])
            self.put(p, a, own, ZP, down, sources[a])
            self.to_core(p, a, 0, 0, sources[a])

    def stage1(self, p):
        up, down, across = neighbour(dz=1), neighbour(dz=-1), neighbour(dh=1)
        self.got(p, 0, self.block(1, 0), Y0)
        self.put(p, 0, self.block(1, 0), YZM, up)
        self.put(p, 0, self.block(1, 0), YZP, down)
        self.to_core(p, 0, 1, 0)
        for a in range(2):
            self.got(p, a, self.block(0, 1), ZP)
            self.put(p, a, self.block(0, 1), FA, down, None, LEFT)
            self.to_core(p, a, 0, 1)
            self.got(p, a, self.block(0, -1), ZM)
            self.put(p, a, self.block(0, -1), FB, up, None, RIGHT)
            self.to_core(p, a, 0, -1)
        self.put(p, 1, self.block(0, 1), YZP, across)
        self.put(p, 1, self.block(0, -1), YZM, across)
        self.got(p, 1, self.block(1, 0), Y0)
        self.to_core(p, 1, 1, 0)

    def stage2(self, p):
        up, down, across = neighbour(dz=1), neighbour(dz=-1), neighbour(dh=1)
        self.got(p, 0, self.block(1, 1), YZP)
        self.put(p, 0, self.block(1, 1), YFA, down, None, LEFT)
        self.to_core(p, 0, 1, 1)
        self.got(p, 0, self.block(1, -1), YZM)
        self.put(p, 0, self.block(1, -1), YFB, up, None, RIGHT)
        self.to_core(p, 0, 1, -1)
        for a in (1, 0):
            self.got(p, a, self.block(0, 2), FA, LEFT)
            self.got(p, a, self.block(0, 2), FB, RIGHT)
            if a == 1:
                self.put(p, 1, self.block(0, 2), YFA, across)
            self.to_core(p, a, 0, 2)
        self.got(p, 1, self.block(1, 1), YZP)
        self.to_core(p, 1, 1, 1)
        self.got(p, 1, self.block(1, -1), YZM)
        self.to_core(p, 1, 1, -1)

    def stage3(self, p):
        self.got(p, 0, self.block(1, 2), YFA, LEFT)
        self.got(p, 0, self.block(1, 2), YFB, RIGHT)
        self.to_core(p, 0, 1, 2)
        self.got(p, 1, self.block(1, 2), YFA)
        self.to_core(p, 1, 1, 2)

    def stage4(self, p):
        for a in range(2):
            for dh in range(2):
                for dz in range(4):
                    rows = self.block(dh, dz, 1)
                    sem = self.core_recv.at[p, a, dh * 4 + dz]
                    self.copy(p, a, rows, sem, neighbour(dc=1)).wait_recv()

    def finish(self, p):
        for a in range(2):
            part = self.bufs[a].at[p, pl.ds(0, 15 * HALF), :]
            pltpu.make_async_copy(part, part, self.send.at[p, a]).wait()


def gather_scratch(pieces):
    return [
        pltpu.SemaphoreType.DMA((pieces, 2)),
        pltpu.SemaphoreType.DMA((pieces, 2, 9)),
        pltpu.SemaphoreType.DMA((pieces, 2, 8)),
    ]


def kernel(
    features, errors, gain, w_in, w_out,
    passed, gain_grad, in_grad, out_grad,
    all_normed, all_errors, acts, win, wout, part, paired, summed, hop1, hop2, total,
    last, in_acc, out_acc, normed, centred, inverses, norm_error, own_error,
    slice_normed, slice_errors, gains,
    send, recv, core_recv, c_send, c_recv, x_send, x_recv, f_send, f_recv, w_sem,
    o_sem, rs_send, rs_recv, g_send, g_recv, p_send, p_recv,
):
    _, d, h, z, c = place()
    up, down, left, right = (
        neighbour(dz=1), neighbour(dz=-1), neighbour(dx=-1), neighbour(dx=1),
    )
    across, other, partner = neighbour(dh=1), neighbour(dc=1), neighbour(ds=1)

    def load_in(k):
        cols = pl.ds(pl.multiple_of(k % 8 * W, W), W)
        return pltpu.make_async_copy(
            w_in.at[cols, :], win.at[k % 3], w_sem.at[0, k % 3]
        )

    def load_out(k):
        cols = pl.ds(pl.multiple_of(k % 8 * W, W), W)
        return pltpu.make_async_copy(
            w_out.at[:, cols], wout.at[k % 2], w_sem.at[1, k % 2]
        )

    for k in range(3):
        load_in(k).start()
    for k in range(2):
        load_out(k).start()

    scale = gain[...]
    for first in range(0, TOK, 16):
        rows = pl.ds(first, 16)
        values = features[rows, :].astype(F32)
        average = jnp.mean(values, -1, keepdims=True)
        values = values - average
        variance = jnp.mean(values * values, -1, keepdims=True)
        inverse = lax.rsqrt(variance + EPSILON)
        values = values * inverse
        centred[rows, :] = values
        inverses[rows, :] = jnp.broadcast_to(inverse, (16, 128))
        normed[rows, :] = (values * scale).astype(BF16)

    gather = Gather((all_normed, all_errors), send, recv, core_recv)
    greet(
        pltpu.get_barrier_semaphore(),
        [up, down, left, right, across, other, partner]
        + [neighbour(dz=2), neighbour(dx=2), neighbour(dh=1, dc=1)],
    )

    def tokens(tau):
        return pl.ds(pl.multiple_of(tau * HALF, HALF), HALF)

    def crossing(g, tau, a):
        dx = (-1, 1, 2)[g]
        cols = pl.ds(pl.multiple_of((d + dx + 4) % 4 * WIDE, WIDE), WIDE)
        return pltpu.make_async_remote_copy(
            src_ref=(normed, errors)[a].at[tokens(tau), cols],
            dst_ref=(slice_normed, slice_errors)[a].at[tau * 3 + g],
            send_sem=c_send.at[tau * 3 + g, a],
            recv_sem=c_recv.at[tau * 3 + g, a],
            device_id=neighbour(dx=dx),
            device_id_type=MESH,
        )

    def stage0(p):
        rows = tokens(p // 4)
        cols = pl.ds(pl.multiple_of(p % 4 * WIDE, WIDE), WIDE)
        gather.stage0(p, (normed.at[rows, cols], errors.at[rows, cols]))
        own = gather.block(0, 0)
        all_normed[p, own, :] = normed[rows, cols]
        all_errors[p, own, :] = errors[rows, cols]

    def stage0_slice(p):
        u = p - PIECES
        for a, buf in enumerate((slice_normed, slice_errors)):
            pltpu.make_async_remote_copy(
                src_ref=buf.at[u],
                dst_ref=buf.at[u],
                send_sem=c_send.at[u, a],
                recv_sem=c_recv.at[u, a],
                device_id=right,
                device_id_type=MESH,
            ).wait_recv()
        gather.stage0(p, (slice_normed.at[u], slice_errors.at[u]))
        own = gather.block(0, 0)
        all_normed[p, own, :] = slice_normed[u]
        all_errors[p, own, :] = slice_errors[u]

    def acting(tau):
        return pl.ds(pl.multiple_of(tau * 256, 256), 256)

    def activate(tau):
        @pl.loop(0, 8)
        def _(i):
            rows = pl.ds(pl.multiple_of(tau * 256 + i * 32, 32), 32)
            x = in_acc[0, rows, :]
            cdf = 0.5 * (1.0 + lax.erf(x * SQRT_HALF))
            density = INV_ROOT_TWO_PI * jnp.exp(-0.5 * x * x)
            acts[1, 3, rows, :] = (x * cdf).astype(BF16)
            acts[0, 3, rows, :] = (in_acc[1, rows, :] * (cdf + x * density)).astype(
                BF16
            )

    def sideways(tau, a, g, part_of):
        rows = pl.ds(pl.multiple_of(tau * 256 + part_of * 128, 128), 128)
        return pltpu.make_async_remote_copy(
            src_ref=acts.at[a, 3, rows, :],
            dst_ref=acts.at[a, g, rows, :],
            send_sem=x_send.at[tau, a, g, part_of],
            recv_sem=x_recv.at[tau, a, g, part_of],
            device_id=(left, right)[g],
            device_id_type=MESH,
        )

    def onward(tau, a, g):
        rows = pl.ds(pl.multiple_of(tau * 256 + g * 128, 128), 128)
        return pltpu.make_async_remote_copy(
            src_ref=acts.at[a, g, rows, :],
            dst_ref=acts.at[a, 2, rows, :],
            send_sem=f_send.at[tau, a, g],
            recv_sem=f_recv.at[tau, a, g],
            device_id=(left, right)[g],
            device_id_type=MESH,
        )

    def each(act):
        for a in range(2):
            for g in range(2):
                act(a, g)

    def move(k, q, source, target_ref, target):
        return pltpu.make_async_remote_copy(
            src_ref=source,
            dst_ref=target_ref,
            send_sem=rs_send.at[q, k],
            recv_sem=rs_recv.at[q, k],
            device_id=target,
            device_id_type=MESH,
        )

    zp, zm, zz = (z + 1) % 4, (z + 3) % 4, (z + 2) % 4

    def m0(q):
        return move(0, q, part.at[q % 3, :, :, 1 - c], paired.at[q], other)

    def m1(q):
        return move(1, q, summed.at[q, :, zz, :, LEFT], hop1.at[q, 0], up)

    def m2(q):
        return move(2, q, summed.at[q, :, zz, :, RIGHT], hop1.at[q, 1], down)

    def m3(q):
        return move(3, q, summed.at[q, :, zp], hop2.at[q, 0], up)

    def m4(q):
        return move(4, q, summed.at[q, :, zm], hop2.at[q, 1], down)

    def m5(q):
        return move(5, q, total.at[q, 1 - h], last.at[q], across)

    def scatter1(q):
        m0(q).wait_recv()
        for hh in range(2):
            for zi in range(4):
                summed[q, hh, zi] = (
                    part[q % 3, hh, zi, c].astype(F32) + paired[q, hh, zi].astype(F32)
                ).astype(BF16)
        m1(q).start()
        m2(q).start()

    def scatter2(q):
        for k, row, cols, came, go in (
            (0, zp, LEFT, m1, m3), (1, zm, RIGHT, m2, m4),
        ):
            came(q).wait_recv()
            for hh in range(2):
                summed[q, hh, row, :, cols] = (
                    summed[q, hh, row, :, cols].astype(F32)
                    + hop1[q, k, hh].astype(F32)
                ).astype(BF16)
            go(q).start()

    def scatter3(q):
        m3(q).wait_recv()
        m4(q).wait_recv()
        for hh in range(2):
            total[q, hh] = (
                summed[q, hh, z].astype(F32)
                + hop2[q, 0, hh].astype(F32)
                + hop2[q, 1, hh].astype(F32)
            ).astype(BF16)
        m5(q).start()

    def scatter4(q):
        m5(q).wait_recv()
        cols = pl.ds(pl.multiple_of(q % 4 * WIDE, WIDE), WIDE)
        norm_error[tokens(q // 4), cols] = total[q, h].astype(F32) + last[q].astype(F32)

    def products(u, g, tau, half):
        cols = (LEFT, RIGHT)[half] if isinstance(half, int) else pl.ds(
            pl.multiple_of(half * W, W), W
        )
        rows = acting(tau)
        return (
            dot(all_normed[u, :, cols], acts[0, g, rows, :], 0, 0),
            dot(acts[1, g, rows, :], all_errors[u, :, cols], 0, 0),
        )

    def add_products(u, g, tau, half):
        to_in, to_out = products(u, g, tau, half)
        in_acc[half] += to_in
        out_acc[half] += to_out

    def correct(tau):
        rows = tokens(tau)
        scaled = norm_error[rows, :] * scale
        around = centred[rows, :]
        shift = jnp.mean(scaled, -1, keepdims=True)
        slope = jnp.mean(scaled * around, -1, keepdims=True)
        corrected = inverses[rows, pl.ds(0, 1)] * (scaled - shift - around * slope)
        own_error[rows, :] = (errors[rows, :].astype(F32) + corrected).astype(BF16)
        swap(tau).start()

    def swap(tau):
        return pltpu.make_async_remote_copy(
            src_ref=own_error.at[tokens(tau), :],
            dst_ref=passed.at[tokens(tau), :],
            send_sem=p_send.at[tau],
            recv_sem=p_recv.at[tau],
            device_id=partner,
            device_id_type=MESH,
        )

    def spread(level, k):
        target, slot = (
            ((neighbour(dc=1), neighbour(dh=1), neighbour(dh=1, dc=1))[k], h * 2 + c),
            (neighbour(dz=k + 1), z),
            (neighbour(dx=k + 1), d),
        )[level]
        return pltpu.make_async_remote_copy(
            src_ref=gains.at[level, slot],
            dst_ref=gains.at[level, slot],
            send_sem=g_send.at[level, k],
            recv_sem=g_recv.at[level, k],
            device_id=target,
            device_id_type=MESH,
        )

    def collect(level):
        for k in range(3):
            spread(level, k).wait_recv()
        value = gains[level, 0] + gains[level, 1] + gains[level, 2] + gains[level, 3]
        if level == 2:
            gain_grad[...] = value
            return
        gains[level + 1, (z, d)[level]] = value
        for k in range(3):
            spread(level + 1, k).start()

    def start_gain():
        for q in range(PIECES):
            cols = pl.ds(q * W, W)
            product = norm_error[:, cols] * centred[:, cols]
            mine = jnp.sum(product, 0, keepdims=True)
            gains[0, h * 2 + c, pl.ds(q, 1), :] = mine
        for k in range(3):
            spread(0, k).start()

    @pl.loop(0, 21)
    def _(t):
        @pl.when((t == 8) | (t == 12))
        def _():
            tau = t // 4 - 2
            activate(tau)
            each(lambda a, g: sideways(tau, a, g, g).start())
            each(lambda a, g: sideways(tau, a, g, 1 - g).start())

        @pl.when(t < PIECES)
        def _():
            stage0(t)

        @pl.when(t == 0)
        def _():
            for tau in range(2):
                for g in range(3):
                    for a in range(2):
                        crossing(g, tau, a).start()

        @pl.when((t >= 1) & (t < PIECES + 1))
        def _():
            gather.stage1(t - 1)

        @pl.when((t >= 2) & (t < PIECES + 2))
        def _():
            gather.stage2(t - 2)

        @pl.when((t >= 3) & (t < PIECES + 3))
        def _():
            gather.stage3(t - 3)

        @pl.when((t >= 4) & (t < PIECES + 4))
        def _():
            gather.stage4(t - 4)

        @pl.when(t >= 11)
        def _():
            @pl.when(t < 16)
            def _():
                m0(t - 11).wait_send()

        @pl.when((t >= 4) & (t < 16))
        def _():
            @pl.loop(0, 2)
            def _(half):
                k = (t - 4) * 2 + half
                cols = pl.ds(pl.multiple_of(half * W, W), W)
                load_in(k).wait()

                @pl.when(t < PIECES + 4)
                def _():
                    p = t - 4
                    load_out(k).wait()
                    pre = dot(all_normed[p, :, cols], win[k % 3], 1, 0)
                    back = dot(all_errors[p, :, cols], wout[k % 2], 1, 1)
                    rows = acting(p // 4)

                    @pl.when(k % 8 == 0)
                    def _():
                        in_acc[0, rows, :] = pre
                        in_acc[1, rows, :] = back

                    @pl.when(k % 8 > 0)
                    def _():
                        in_acc[0, rows, :] += pre
                        in_acc[1, rows, :] += back

                    @pl.when(k < 14)
                    def _():
                        load_out(k + 2).start()

                @pl.when(t >= 8)
                def _():
                    q = t - 8
                    known = acts[0, 3, acting(q // 4), :]
                    value = dot(known, win[k % 3], 1, 1).astype(BF16)
                    part[q % 3, :, :, :, :, cols] = value.reshape(2, 4, 2, HALF, W)

                @pl.when(k < 21)
                def _():
                    load_in(k + 3).start()

            @pl.when(t >= 8)
            def _():
                m0(t - 8).start()

        @pl.when((t >= 9) & (t < 17))
        def _():
            scatter1(t - 9)

        @pl.when((t >= 10) & (t < 18))
        def _():
            scatter2(t - 10)

        @pl.when((t >= 11) & (t < 19))
        def _():
            scatter3(t - 11)

        @pl.when((t >= 12) & (t < 20))
        def _():
            scatter4(t - 12)

        @pl.when(((t >= 9) & (t < 12)) | ((t >= 14) & (t < 17)))
        def _():
            stage0_slice(t - 1 - 2 * (t // 13))

        @pl.when(((t >= 10) & (t < 13)) | ((t >= 16) & (t < 19)))
        def _():
            gather.stage1(t - 2 - 3 * (t // 16))

        @pl.when(((t >= 11) & (t < 14)) | ((t >= 17) & (t < 20)))
        def _():
            gather.stage2(t - 3 - 3 * (t // 17))

        @pl.when(((t >= 12) & (t < 15)) | (t >= 18))
        def _():
            gather.stage3(t - 4 - 3 * (t // 18))

        @pl.when((t == 10) | (t == 14))
        def _():
            tau = (t - 10) // 4
            each(lambda a, g: sideways(tau, a, g, g).wait_recv())
            each(lambda a, g: onward(tau, a, g).start())

        @pl.when((t == 14) | (t == 18))
        def _():
            tau = (t - 14) // 4
            each(lambda a, g: sideways(tau, a, g, 1 - g).wait_recv())

        @pl.when(t == 16)
        def _():
            each(lambda a, g: onward(0, a, g).wait_recv())
            correct(0)

        @pl.when((t == 12) | (t == 13))
        def _():
            tau = t - 12

            @pl.loop(0, 2)
            def _(half):
                to_in, to_out = products(tau * 4 + d, 3, tau, half)

                @pl.when(tau == 0)
                def _():
                    in_acc[half] = to_in
                    out_acc[half] = to_out

                @pl.when(tau == 1)
                def _():
                    in_acc[half] += to_in
                    out_acc[half] += to_out

        @pl.when(t == 19)
        def _():
            start_gain()
            correct(1)

        @pl.when(t == 20)
        def _():
            collect(0)

        @pl.when(((t >= 15) & (t < 18)) | (t >= 19))
        def _():
            u = t - 15 - t // 19
            gather.stage4(PIECES + u)

            @pl.loop(0, 2)
            def _(half):
                add_products(PIECES + u, u % 3, u // 3, half)

    each(lambda a, g: onward(1, a, g).wait_recv())
    gather.stage4(13)

    def emit(half):
        part_of = pl.ds(pl.multiple_of(half * W, W), W)
        return (
            pltpu.make_async_copy(win.at[0], in_grad.at[part_of, :], o_sem.at[0]),
            pltpu.make_async_copy(win.at[1], out_grad.at[:, part_of], o_sem.at[1]),
        )

    @pl.loop(0, 2)
    def _(half):
        add_products(13, 2, 1, half)

        @pl.when(half == 1)
        def _():
            for copy in emit(0):
                copy.wait()

        win[0] = in_acc[half].astype(BF16)
        win[1] = out_acc[half].astype(BF16)
        for copy in emit(half):
            copy.start()

        @pl.when(half == 0)
        def _():
            collect(1)

    for tau in range(2):
        for g in range(3):
            for a in range(2):
                crossing(g, tau, a).wait_send()
        each(lambda a, g: sideways(tau, a, g, 0).wait_send())
        each(lambda a, g: sideways(tau, a, g, 1).wait_send())
        each(lambda a, g: onward(tau, a, g).wait_send())

    @pl.loop(0, ALL)
    def _(p):
        gather.finish(p)

    @pl.loop(0, PIECES)
    def _(q):
        @pl.when(q >= 5)
        def _():
            m0(q).wait_send()

        for m in (m1, m2, m3, m4, m5):
            m(q).wait_send()

    collect(2)
    for level in range(3):
        for k in range(3):
            spread(level, k).wait_send()
    for tau in range(2):
        swap(tau).wait()
    for copy in emit(1):
        copy.wait()


def shape(dims, dtype=BF16):
    return jax.ShapeDtypeStruct(dims, dtype)


VM = pl.BlockSpec(memory_space=pltpu.VMEM)
ANY = pl.BlockSpec(memory_space=pl.ANY)
DMA = pltpu.SemaphoreType.DMA


def block_call(features, errors, gain, w_in, w_out):
    bf16, f32 = functools.partial(pltpu.VMEM, dtype=BF16), functools.partial(
        pltpu.VMEM, dtype=F32
    )
    return pl.pallas_call(
        kernel,
        name="block",
        out_shape=(
            shape((TOK, W * PIECES)), shape((8, W), F32),
            shape((2 * W, W)), shape((W, 2 * W)),
        ),
        in_specs=[VM, VM, VM, ANY, ANY],
        out_specs=(ANY, VM, ANY, ANY),
        scratch_shapes=[
            bf16((ALL, 16 * HALF, WIDE)),
            bf16((ALL, 16 * HALF, WIDE)),
            bf16((2, 4, GROUP, W)),
            bf16((3, W, W)),
            bf16((2, W, W)),
            bf16((3, 2, 4, 2, HALF, WIDE)),
            bf16((PIECES, 2, 4, HALF, WIDE)),
            bf16((PIECES, 2, 4, HALF, WIDE)),
            bf16((PIECES, 2, 2, HALF, W)),
            bf16((PIECES, 2, 2, HALF, WIDE)),
            bf16((PIECES, 2, HALF, WIDE)),
            bf16((PIECES, HALF, WIDE)),
            f32((2, W, W)),
            f32((2, W, W)),
            bf16((TOK, W * PIECES)),
            f32((TOK, W * PIECES)),
            f32((TOK, 128)),
            f32((TOK, W * PIECES)),
            bf16((TOK, W * PIECES)),
            bf16((6, HALF, WIDE)),
            bf16((6, HALF, WIDE)),
            f32((3, 4, 8, W)),
            *gather_scratch(ALL),
            DMA((6, 2)), DMA((6, 2)), DMA((2, 2, 2, 2)), DMA((2, 2, 2, 2)),
            DMA((2, 2, 2)), DMA((2, 2, 2)), DMA((2, 3)), DMA((2,)),
            DMA((PIECES, 6)), DMA((PIECES, 6)), DMA((3, 3)), DMA((3, 3)),
            DMA((2,)), DMA((2,)),
        ],
        compiler_params=pltpu.CompilerParams(
            collective_id=0, has_side_effects=True, vmem_limit_bytes=LIMIT
        ),
    )(features, errors, gain, w_in, w_out)


def emit_kernel(
    passed, gain, in_grad, out_grad,
    passed_out, gain_out, in_out, out_out,
    a, b, load, save,
):
    pairs = []
    for k in range(4):
        rows = pl.ds(k * 384, 384)
        pairs.append((in_grad.at[rows, :], a.at[rows, :], in_out.at[rows, :]))
        rows = pl.ds(k * 192, 192)
        pairs.append((out_grad.at[rows, :], b.at[rows, :], out_out.at[rows, :]))
    pairs.append((passed, passed_out, None))
    loads = [
        pltpu.make_async_copy(source, held, load.at[k])
        for k, (source, held, _) in enumerate(pairs)
    ]
    for copy in loads:
        copy.start()
    for q in range(PIECES):
        gain_out[:, pl.ds(q * W, W)] = gain[pl.ds(q, 1), :]
    saves = []
    for k, (_, held, out) in enumerate(pairs):
        loads[k].wait()
        if out is not None:
            saves.append(pltpu.make_async_copy(held, out, save.at[k]))
            saves[-1].start()
    for copy in saves:
        copy.wait()


def emit_call(*results):
    return pl.pallas_call(
        emit_kernel,
        name="emit",
        out_shape=(
            shape((TOK, W * PIECES)), shape((1, W * PIECES), F32),
            shape((2 * W, W)), shape((W, 2 * W)),
        ),
        in_specs=[ANY, VM, ANY, ANY],
        out_specs=(VM, VM, ANY, ANY),
        scratch_shapes=[
            pltpu.VMEM((WIDE, W), BF16), pltpu.VMEM((W, WIDE), BF16),
            DMA((9,)), DMA((9,)),
        ],
    )(*results)


def per_device(features, delayed_error, ln_gain, w_in, w_out):
    results = block_call(features[0], delayed_error[0], ln_gain, w_in[0], w_out[0])
    passed, gain_grad, in_total, out_total = emit_call(*results)
    return passed[None], gain_grad, in_total[None], out_total[None]


def solution(mesh):
    return jax.shard_map(
        per_device,
        mesh=mesh,
        in_specs=(
            P("section", ("dp", "shard"), None),
            P("section", ("dp", "shard"), None),
            P("section", None),
            P("section", None, "shard"),
            P("section", "shard", None),
        ),
        out_specs=(
            P("section", ("dp", "shard"), None),
            P("section", None),
            P("section", "dp", "shard"),
            P("section", "shard", "dp"),
        ),
        check_vma=False,
    )
```

```python
import functools

import jax
import jax.numpy as jnp
from jax import lax
from jax.experimental import pallas as pl
from jax.experimental.pallas import tpu as pltpu
from jax.sharding import PartitionSpec as P

SQRT_HALF = 0.7071067811865476
INV_ROOT_TWO_PI = 0.3989422804014327
EPSILON = 1e-06
F32 = jnp.float32
BF16 = jnp.bfloat16
MESH = pl.DeviceIdType.MESH
W = 768
WIDE = 2 * W
HALF = 16
TOK = 32
GROUP = 512
PIECES = 8
ALL = 14
LIMIT = 66_900_000

def place():
    s = lax.axis_index("section")
    d = lax.axis_index("dp")
    j = lax.axis_index("shard")
    return s, d, j // 8, (j // 2) % 4, j % 2


def neighbour(dx=0, dh=0, dz=0, dc=0, ds=0):
    s, d, h, z, c = place()
    return (
        (s + ds) % 2,
        (d + dx + 4) % 4,
        ((h + dh) % 2) * 8 + ((z + dz + 4) % 4) * 2 + (c + dc) % 2,
    )


def greet(barrier, targets):
    for target in targets:
        pl.semaphore_signal(barrier, inc=1, device_id=target, device_id_type=MESH)
    pl.semaphore_wait(barrier, len(targets))


def dot(a, b, ca, cb):
    return lax.dot_general(
        a, b, (((ca,), (cb,)), ((), ())), preferred_element_type=F32
    )


FULL, LEFT, RIGHT = pl.ds(0, WIDE), pl.ds(0, W), pl.ds(W, W)


class Gather:
    def __init__(self, bufs, send, recv, core_recv):
        self.bufs, self.send, self.recv, self.core_recv = bufs, send, recv, core_recv

    def block(self, dh, dz, dc=0):
        _, _, h, z, c = place()
        index = ((h + dh) % 2) * 8 + ((z + dz + 4) % 4) * 2 + (c + dc) % 2
        return pl.ds(pl.multiple_of(index * HALF, HALF), HALF)

    def copy(self, p, a, rows, sem, target, source=None, cols=FULL):
        there = self.bufs[a].at[p, rows, cols]
        return pltpu.make_async_remote_copy(
            src_ref=there if source is None else source,
            dst_ref=there,
            send_sem=self.send.at[p, a],
            recv_sem=sem,
            device_id=target,
            device_id_type=MESH,
        )

    def put(self, stage, p, a, rows, target, source=None, cols=FULL):
        sem = self.recv.at[p, a, stage]
        self.copy(p, a, rows, sem, target, source, cols).start()

    def got(self, stage, p, a):
        rows = pl.ds(0, (3, 3, 1)[stage] * HALF)
        sem = self.recv.at[p, a, stage]
        self.copy(p, a, rows, sem, neighbour(dz=1)).wait_recv()

    def to_core(self, p, a, dh, dz, source=None):
        sem = self.core_recv.at[p, a]
        self.copy(p, a, self.block(dh, dz), sem, neighbour(dc=1), source).start()

    def stage0(self, p, sources):
        up, down, across = neighbour(dz=1), neighbour(dz=-1), neighbour(dh=1)
        own = self.block(0, 0)
        for a in range(2):
            self.put(0, p, a, own, across, sources[a])
            self.put(0, p, a, own, up, sources[a])
            self.put(0, p, a, own, down, sources[a])
            self.to_core(p, a, 0, 0, sources[a])

    def stage1(self, p):
        up, down, across = neighbour(dz=1), neighbour(dz=-1), neighbour(dh=1)
        for a in range(2):
            self.got(0, p, a)
            if a == 0:
                self.put(1, p, 0, self.block(1, 0), up)
                self.put(1, p, 0, self.block(1, 0), down)
            else:
                self.put(1, p, 1, self.block(0, 1), across)
                self.put(1, p, 1, self.block(0, -1), across)
            self.put(1, p, a, self.block(0, 1), down, None, LEFT)
            self.put(1, p, a, self.block(0, -1), up, None, RIGHT)
            self.to_core(p, a, 1, 0)
            self.to_core(p, a, 0, 1)
            self.to_core(p, a, 0, -1)

    def stage2(self, p):
        up, down, across = neighbour(dz=1), neighbour(dz=-1), neighbour(dh=1)
        for a in range(2):
            self.got(1, p, a)
            if a == 0:
                self.put(2, p, 0, self.block(1, 1), down, None, LEFT)
                self.put(2, p, 0, self.block(1, -1), up, None, RIGHT)
            else:
                self.put(2, p, 1, self.block(0, 2), across)
            self.to_core(p, a, 1, 1)
            self.to_core(p, a, 1, -1)
            self.to_core(p, a, 0, 2)

    def stage3(self, p):
        for a in range(2):
            self.got(2, p, a)
            self.to_core(p, a, 1, 2)

    def stage4(self, p):
        for a in range(2):
            rows = pl.ds(0, 8 * HALF)
            sem = self.core_recv.at[p, a]
            self.copy(p, a, rows, sem, neighbour(dc=1)).wait_recv()

    def finish(self, p):
        for a in range(2):
            part = self.bufs[a].at[p, pl.ds(0, 15 * HALF), :]
            pltpu.make_async_copy(part, part, self.send.at[p, a]).wait()


def gather_scratch(pieces):
    return [
        pltpu.SemaphoreType.DMA((pieces, 2)),
        pltpu.SemaphoreType.DMA((pieces, 2, 3)),
        pltpu.SemaphoreType.DMA((pieces, 2)),
    ]


def kernel(
    features, errors, gain, w_in, w_out,
    passed, gain_grad, in_grad, out_grad,
    all_normed, all_errors, acts, win, wout, part, paired, summed, hop1, hop2, total,
    last, in_acc, out_acc, normed, centred, inverses, norm_error, own_error,
    slice_normed, slice_errors, gains,
    send, recv, core_recv, c_send, c_recv, x_send, x_recv, w_sem,
    o_sem, rs_send, rs_recv, g_send, g_recv, p_send, p_recv,
):
    _, d, h, z, c = place()
    up, down, left, right = (
        neighbour(dz=1), neighbour(dz=-1), neighbour(dx=-1), neighbour(dx=1),
    )
    across, other, partner = neighbour(dh=1), neighbour(dc=1), neighbour(ds=1)

    def turn(p):
        return (p + d + 1) % 4

    def load_in(k):
        cols = pl.ds(pl.multiple_of(turn(k // 2) * WIDE + k % 2 * W, W), W)
        return pltpu.make_async_copy(
            w_in.at[cols, :], win.at[k % 3], w_sem.at[0, k % 3]
        )

    def load_out(k):
        cols = pl.ds(pl.multiple_of(turn(k // 2) * WIDE + k % 2 * W, W), W)
        return pltpu.make_async_copy(
            w_out.at[:, cols], wout.at[k % 2], w_sem.at[1, k % 2]
        )

    for k in range(3):
        load_in(k).start()
    for k in range(2):
        load_out(k).start()

    scale = gain[...]
    for first in range(0, TOK, 16):
        rows = pl.ds(first, 16)
        values = features[rows, :].astype(F32)
        average = jnp.mean(values, -1, keepdims=True)
        values = values - average
        variance = jnp.mean(values * values, -1, keepdims=True)
        inverse = lax.rsqrt(variance + EPSILON)
        values = values * inverse
        centred[rows, :] = values
        inverses[rows, :] = jnp.broadcast_to(inverse, (16, 128))
        normed[rows, :] = (values * scale).astype(BF16)

    gather = Gather((all_normed, all_errors), send, recv, core_recv)
    greet(
        pltpu.get_barrier_semaphore(),
        [up, down, left, right, across, other, partner]
        + [neighbour(dz=2), neighbour(dx=2), neighbour(dh=1, dc=1)],
    )

    def tokens(tau):
        return pl.ds(pl.multiple_of(tau * HALF, HALF), HALF)

    def crossing(g, tau, a):
        dx = (-1, 1, 2)[g]
        cols = pl.ds(pl.multiple_of((d + dx + 4) % 4 * WIDE, WIDE), WIDE)
        return pltpu.make_async_remote_copy(
            src_ref=(normed, errors)[a].at[tokens(tau), cols],
            dst_ref=(slice_normed, slice_errors)[a].at[tau * 3 + g],
            send_sem=c_send,
            recv_sem=c_recv.at[tau * 3 + g, a],
            device_id=neighbour(dx=dx),
            device_id_type=MESH,
        )

    def stage0(p):
        rows = tokens(p // 4)
        cols = pl.ds(pl.multiple_of(turn(p) * WIDE, WIDE), WIDE)
        gather.stage0(p, (normed.at[rows, cols], errors.at[rows, cols]))
        own = gather.block(0, 0)
        all_normed[p, own, :] = normed[rows, cols]
        all_errors[p, own, :] = errors[rows, cols]

    def stage0_slice(p):
        u = p - PIECES
        for a, buf in enumerate((slice_normed, slice_errors)):
            pltpu.make_async_remote_copy(
                src_ref=buf.at[u],
                dst_ref=buf.at[u],
                send_sem=c_send,
                recv_sem=c_recv.at[u, a],
                device_id=right,
                device_id_type=MESH,
            ).wait_recv()
        gather.stage0(p, (slice_normed.at[u], slice_errors.at[u]))
        own = gather.block(0, 0)
        all_normed[p, own, :] = slice_normed[u]
        all_errors[p, own, :] = slice_errors[u]

    def hand(p, g, act):
        for a, buf in enumerate((all_normed, all_errors)):
            for i in range(8):
                rows = pl.ds(pl.multiple_of((i * 2 + c) * HALF, HALF), HALF)
                act(
                    pltpu.make_async_remote_copy(
                        src_ref=buf.at[p, rows, :],
                        dst_ref=buf.at[PIECES + g, rows, :],
                        send_sem=send.at[PIECES + g, a],
                        recv_sem=recv.at[PIECES + g, a, 0],
                        device_id=(left, right)[g],
                        device_id_type=MESH,
                    )
                )

    def handed(g):
        for a, buf in enumerate((all_normed, all_errors)):
            there = buf.at[PIECES + g, pl.ds(0, 8 * HALF), :]
            pltpu.make_async_copy(there, there, recv.at[PIECES + g, a, 0]).wait()
            for i in range(8):
                rows = pl.ds(pl.multiple_of((i * 2 + c) * HALF, HALF), HALF)
                pltpu.make_async_remote_copy(
                    src_ref=buf.at[PIECES + g, rows, :],
                    dst_ref=buf.at[PIECES + g, rows, :],
                    send_sem=send.at[PIECES + g, a],
                    recv_sem=core_recv.at[PIECES + g, a],
                    device_id=other,
                    device_id_type=MESH,
                ).start()

    def acting(tau):
        return pl.ds(pl.multiple_of(tau * 256, 256), 256)

    def activate(tau):
        @pl.loop(0, 8)
        def _(i):
            rows = pl.ds(pl.multiple_of(tau * 256 + i * 32, 32), 32)
            x = in_acc[0, rows, :]
            cdf = 0.5 * (1.0 + lax.erf(x * SQRT_HALF))
            density = INV_ROOT_TWO_PI * jnp.exp(-0.5 * x * x)
            acts[1, 3, rows, :] = (x * cdf).astype(BF16)
            acts[0, 3, rows, :] = (in_acc[1, rows, :] * (cdf + x * density)).astype(
                BF16
            )

    def sideways(tau, a, g, part_of):
        rows = pl.ds(pl.multiple_of(tau * 256 + part_of * 128, 128), 128)
        return pltpu.make_async_remote_copy(
            src_ref=acts.at[a, 3, rows, :],
            dst_ref=acts.at[a, g, rows, :],
            send_sem=x_send.at[tau],
            recv_sem=x_recv.at[tau, (part_of + g) % 2],
            device_id=(left, right)[g],
            device_id_type=MESH,
        )

    def onward(tau, a, g):
        rows = pl.ds(pl.multiple_of(tau * 256 + g * 128, 128), 128)
        return pltpu.make_async_remote_copy(
            src_ref=acts.at[a, g, rows, :],
            dst_ref=acts.at[a, 2, rows, :],
            send_sem=x_send.at[tau],
            recv_sem=x_recv.at[tau, 2],
            device_id=(left, right)[g],
            device_id_type=MESH,
        )

    def arrived(tau, k):
        there = acts.at[0, 0]
        pltpu.make_async_copy(there, there, x_recv.at[tau, k]).wait()

    def each(act):
        for a in range(2):
            for g in range(2):
                act(a, g)

    def move(k, q, source, target_ref, target):
        return pltpu.make_async_remote_copy(
            src_ref=source,
            dst_ref=target_ref,
            send_sem=rs_send.at[q, min(k, 1)],
            recv_sem=rs_recv.at[q, (k + 1) // 2],
            device_id=target,
            device_id_type=MESH,
        )

    zp, zm, zz = (z + 1) % 4, (z + 3) % 4, (z + 2) % 4

    def m0(q):
        return move(0, q, part.at[q % 3, :, :, 1 - c], paired.at[q], other)

    def m1(q):
        return move(1, q, summed.at[q, :, zz, :, LEFT], hop1.at[q, 0], up)

    def m2(q):
        return move(2, q, summed.at[q, :, zz, :, RIGHT], hop1.at[q, 1], down)

    def m3(q):
        return move(3, q, summed.at[q, :, zp], hop2.at[q, 0], up)

    def m4(q):
        return move(4, q, summed.at[q, :, zm], hop2.at[q, 1], down)

    def m5(q):
        return move(5, q, total.at[q, 1 - h], last.at[q], across)

    def scatter1(q):
        m0(q).wait_recv()
        for hh in range(2):
            for zi in range(4):
                summed[q, hh, zi] = (
                    part[q % 3, hh, zi, c].astype(F32) + paired[q, hh, zi].astype(F32)
                ).astype(BF16)
        m1(q).start()
        m2(q).start()

    def both(q, k, count):
        there = hop2.at[q, pl.ds(0, count)]
        pltpu.make_async_copy(there, there, rs_recv.at[q, k]).wait()

    def scatter2(q):
        both(q, 1, 1)
        for k, row, cols, go in ((0, zp, LEFT, m3), (1, zm, RIGHT, m4)):
            for hh in range(2):
                summed[q, hh, row, :, cols] = (
                    summed[q, hh, row, :, cols].astype(F32)
                    + hop1[q, k, hh].astype(F32)
                ).astype(BF16)
            go(q).start()

    def scatter3(q):
        both(q, 2, 2)
        for hh in range(2):
            total[q, hh] = (
                summed[q, hh, z].astype(F32)
                + hop2[q, 0, hh].astype(F32)
                + hop2[q, 1, hh].astype(F32)
            ).astype(BF16)
        m5(q).start()

    def scatter4(q):
        m5(q).wait_recv()
        cols = pl.ds(pl.multiple_of(turn(q) * WIDE, WIDE), WIDE)
        norm_error[tokens(q // 4), cols] = total[q, h].astype(F32) + last[q].astype(F32)

    def products(u, g, tau, half):
        cols = (LEFT, RIGHT)[half] if isinstance(half, int) else pl.ds(
            pl.multiple_of(half * W, W), W
        )
        rows = acting(tau)
        return (
            dot(all_normed[u, :, cols], acts[0, g, rows, :], 0, 0),
            dot(acts[1, g, rows, :], all_errors[u, :, cols], 0, 0),
        )

    def add_products(u, g, tau, half):
        to_in, to_out = products(u, g, tau, half)
        in_acc[half] += to_in
        out_acc[half] += to_out

    def correct(tau):
        rows = tokens(tau)
        scaled = norm_error[rows, :] * scale
        around = centred[rows, :]
        shift = jnp.mean(scaled, -1, keepdims=True)
        slope = jnp.mean(scaled * around, -1, keepdims=True)
        corrected = inverses[rows, pl.ds(0, 1)] * (scaled - shift - around * slope)
        own_error[rows, :] = (errors[rows, :].astype(F32) + corrected).astype(BF16)
        swap(tau).start()

    def swap(tau):
        return pltpu.make_async_remote_copy(
            src_ref=own_error.at[tokens(tau), :],
            dst_ref=passed.at[tokens(tau), :],
            send_sem=p_send.at[tau],
            recv_sem=p_recv.at[tau],
            device_id=partner,
            device_id_type=MESH,
        )

    def spread(level, k):
        target, slot = (
            ((neighbour(dc=1), neighbour(dh=1), neighbour(dh=1, dc=1))[k], h * 2 + c),
            (neighbour(dz=k + 1), z),
            (neighbour(dx=k + 1), d),
        )[level]
        return pltpu.make_async_remote_copy(
            src_ref=gains.at[level, slot],
            dst_ref=gains.at[level, slot],
            send_sem=g_send.at[level],
            recv_sem=g_recv.at[level],
            device_id=target,
            device_id_type=MESH,
        )

    def collect(level):
        there = gains.at[level, pl.ds(0, 3)]
        pltpu.make_async_copy(there, there, g_recv.at[level]).wait()
        value = gains[level, 0] + gains[level, 1] + gains[level, 2] + gains[level, 3]
        if level == 2:
            for q in range(PIECES):
                gain_grad[:, pl.ds(q * W, W)] = value[q : q + 1, :]
            return
        gains[level + 1, (z, d)[level]] = value
        for k in range(3):
            spread(level + 1, k).start()

    def start_gain():
        for q in range(PIECES):
            cols = pl.ds(q * W, W)
            product = norm_error[:, cols] * centred[:, cols]
            mine = jnp.sum(product, 0, keepdims=True)
            gains[0, h * 2 + c, pl.ds(q, 1), :] = mine
        for k in range(3):
            spread(0, k).start()

    @pl.loop(0, 20)
    def _(t):
        @pl.when((t == 8) | (t == 12))
        def _():
            tau = t // 4 - 2
            activate(tau)
            each(lambda a, g: sideways(tau, a, g, g).start())
            each(lambda a, g: sideways(tau, a, g, 1 - g).start())

        @pl.when(t < PIECES)
        def _():
            stage0(t)

        @pl.when(t == 0)
        def _():
            for tau, g in ((0, 2), (1, 0), (1, 1), (1, 2)):
                for a in range(2):
                    crossing(g, tau, a).start()

        @pl.when((t >= 1) & (t < PIECES + 1))
        def _():
            gather.stage1(t - 1)

        @pl.when((t >= 2) & (t < PIECES + 2))
        def _():
            gather.stage2(t - 2)

        @pl.when((t >= 3) & (t < PIECES + 3))
        def _():
            gather.stage3(t - 3)

        @pl.when((t >= 4) & (t < PIECES + 4))
        def _():
            gather.stage4(t - 4)

        @pl.when(t == 4)
        def _():
            hand(0, 1, lambda copy: copy.start())

        @pl.when(t == 6)
        def _():
            hand(2, 0, lambda copy: copy.start())

        @pl.when(t >= 11)
        def _():
            @pl.when(t < 16)
            def _():
                m0(t - 11).wait_send()

        @pl.when((t >= 4) & (t < 16))
        def _():
            @pl.loop(0, 2)
            def _(half):
                k = (t - 4) * 2 + half
                cols = pl.ds(pl.multiple_of(half * W, W), W)
                load_in(k).wait()

                @pl.when(t < PIECES + 4)
                def _():
                    p = t - 4
                    load_out(k).wait()
                    pre = dot(all_normed[p, :, cols], win[k % 3], 1, 0)
                    back = dot(all_errors[p, :, cols], wout[k % 2], 1, 1)
                    rows = acting(p // 4)

                    @pl.when(k % 8 == 0)
                    def _():
                        in_acc[0, rows, :] = pre
                        in_acc[1, rows, :] = back

                    @pl.when(k % 8 > 0)
                    def _():
                        in_acc[0, rows, :] += pre
                        in_acc[1, rows, :] += back

                    @pl.when(k < 14)
                    def _():
                        load_out(k + 2).start()

                @pl.when(t >= 8)
                def _():
                    q = t - 8
                    known = acts[0, 3, acting(q // 4), :]
                    value = dot(known, win[k % 3], 1, 1).astype(BF16)
                    part[q % 3, :, :, :, :, cols] = value.reshape(2, 4, 2, HALF, W)

                @pl.when(k < 21)
                def _():
                    load_in(k + 3).start()

            @pl.when(t >= 8)
            def _():
                m0(t - 8).start()

        @pl.when((t >= 9) & (t < 17))
        def _():
            scatter1(t - 9)

        @pl.when((t >= 10) & (t < 18))
        def _():
            scatter2(t - 10)

        @pl.when((t >= 11) & (t < 19))
        def _():
            scatter3(t - 11)

        @pl.when((t >= 12) & (t < 20))
        def _():
            scatter4(t - 12)

        @pl.when((t == 9) | ((t >= 13) & (t < 16)))
        def _():
            stage0_slice(t + 1 - 3 * (t // 13))

        @pl.when((t == 10) | ((t >= 15) & (t < 18)))
        def _():
            gather.stage1(t - 4 * (t // 15))

        @pl.when((t == 11) | ((t >= 16) & (t < 19)))
        def _():
            gather.stage2(t - 1 - 4 * (t // 16))

        @pl.when((t == 12) | (t >= 17))
        def _():
            gather.stage3(t - 2 - 4 * (t // 17))

        @pl.when(t == 10)
        def _():
            handed(1)

        @pl.when(t == 12)
        def _():
            handed(0)

        @pl.when((t == 12) | (t == 15))
        def _():
            tau = (t - 12) // 3
            arrived(tau, 0)
            each(lambda a, g: onward(tau, a, g).start())

        @pl.when((t == 14) | (t == 18))
        def _():
            tau = (t - 14) // 4
            arrived(tau, 1)

        @pl.when(t == 16)
        def _():
            arrived(0, 2)
            correct(0)

        @pl.when((t == 12) | (t == 13))
        def _():
            tau = t - 12

            @pl.loop(0, 2)
            def _(half):
                to_in, to_out = products(tau * 4 + 3, 3, tau, half)

                @pl.when(tau == 0)
                def _():
                    in_acc[half] = to_in
                    out_acc[half] = to_out

                @pl.when(tau == 1)
                def _():
                    in_acc[half] += to_in
                    out_acc[half] += to_out

        @pl.when(t == 19)
        def _():
            start_gain()
            correct(1)

        @pl.when(t >= 15)
        def _():
            u = t - 15
            gather.stage4(PIECES + u)

            @pl.loop(0, 2)
            def _(half):
                add_products(PIECES + u, u % 3, u // 3, half)

    collect(0)
    arrived(1, 2)
    gather.stage4(13)

    def emit(half):
        part_of = pl.ds(pl.multiple_of(half * W, W), W)
        return (
            pltpu.make_async_copy(win.at[0], in_grad.at[part_of, :], o_sem.at[0]),
            pltpu.make_async_copy(win.at[1], out_grad.at[:, part_of], o_sem.at[1]),
        )

    @pl.loop(0, 2)
    def _(half):
        add_products(13, 2, 1, half)

        @pl.when(half == 1)
        def _():
            for copy in emit(0):
                copy.wait()

        win[0] = in_acc[half].astype(BF16)
        win[1] = out_acc[half].astype(BF16)
        for copy in emit(half):
            copy.start()

        @pl.when(half == 0)
        def _():
            collect(1)

    part_of = all_normed.at[0, pl.ds(0, 8 * HALF), :]
    pltpu.make_async_copy(part_of, part_of, c_send).wait()
    for tau in range(2):
        part_of = acts.at[0, pl.ds(0, 3)]
        pltpu.make_async_copy(part_of, part_of, x_send.at[tau]).wait()

    @pl.loop(0, ALL)
    def _(p):
        @pl.when((p < PIECES) | (p >= PIECES + 2))
        def _():
            gather.finish(p)

        @pl.when((p >= PIECES) & (p < PIECES + 2))
        def _():
            for a, buf in enumerate((all_normed, all_errors)):
                there = buf.at[p]
                pltpu.make_async_copy(there, there, send.at[p, a]).wait()

    @pl.loop(0, PIECES)
    def _(q):
        @pl.when(q >= 5)
        def _():
            m0(q).wait_send()

        part_of = all_normed.at[0, pl.ds(0, 7 * HALF), :]
        pltpu.make_async_copy(part_of, part_of, rs_send.at[q, 1]).wait()

    collect(2)
    for level in range(3):
        there = gains.at[level, pl.ds(0, 3)]
        pltpu.make_async_copy(there, there, g_send.at[level]).wait()
    for tau in range(2):
        swap(tau).wait()
    for copy in emit(1):
        copy.wait()


def shape(dims, dtype=BF16):
    return jax.ShapeDtypeStruct(dims, dtype)


VM = pl.BlockSpec(memory_space=pltpu.VMEM)
ANY = pl.BlockSpec(memory_space=pl.ANY)
DMA = pltpu.SemaphoreType.DMA


def block_call(features, errors, gain, w_in, w_out):
    bf16, f32 = functools.partial(pltpu.VMEM, dtype=BF16), functools.partial(
        pltpu.VMEM, dtype=F32
    )
    return pl.pallas_call(
        kernel,
        name="block",
        out_shape=(
            shape((TOK, W * PIECES)), shape((1, W * PIECES), F32),
            shape((2 * W, W)), shape((W, 2 * W)),
        ),
        in_specs=[VM, VM, VM, ANY, ANY],
        out_specs=(ANY, VM, ANY, ANY),
        scratch_shapes=[
            bf16((ALL, 16 * HALF, WIDE)),
            bf16((ALL, 16 * HALF, WIDE)),
            bf16((2, 4, GROUP, W)),
            bf16((3, W, W)),
            bf16((2, W, W)),
            bf16((3, 2, 4, 2, HALF, WIDE)),
            bf16((PIECES, 2, 4, HALF, WIDE)),
            bf16((PIECES, 2, 4, HALF, WIDE)),
            bf16((PIECES, 2, 2, HALF, W)),
            bf16((PIECES, 2, 2, HALF, WIDE)),
            bf16((PIECES, 2, HALF, WIDE)),
            bf16((PIECES, HALF, WIDE)),
            f32((2, W, W)),
            f32((2, W, W)),
            bf16((TOK, W * PIECES)),
            f32((TOK, W * PIECES)),
            f32((TOK, 128)),
            f32((TOK, W * PIECES)),
            bf16((TOK, W * PIECES)),
            bf16((6, HALF, WIDE)),
            bf16((6, HALF, WIDE)),
            f32((3, 4, 8, W)),
            *gather_scratch(ALL),
            DMA, DMA((6, 2)), DMA((2,)), DMA((2, 3)), DMA((2, 3)), DMA((2,)),
            DMA((PIECES, 2)), DMA((PIECES, 4)), DMA((3,)), DMA((3,)),
            DMA((2,)), DMA((2,)),
        ],
        compiler_params=pltpu.CompilerParams(
            collective_id=0, has_side_effects=True, vmem_limit_bytes=LIMIT
        ),
    )(features, errors, gain, w_in, w_out)


def emit_kernel(
    passed, gain, in_grad, out_grad,
    passed_out, gain_out, in_out, out_out,
    a, b, held_passed, held_gain, load, save,
):
    pairs = []
    for k in range(4):
        rows = pl.ds(k * 384, 384)
        pairs.append((in_grad.at[rows, :], a.at[rows, :], in_out.at[rows, :]))
        rows = pl.ds(k * 192, 192)
        pairs.append((out_grad.at[rows, :], b.at[rows, :], out_out.at[rows, :]))
    pairs.append((passed, held_passed, passed_out))
    pairs.append((gain, held_gain, gain_out))
    loads = [
        pltpu.make_async_copy(source, held, load.at[k])
        for k, (source, held, _) in enumerate(pairs)
    ]
    for copy in loads:
        copy.start()
    saves = []
    for k, (_, held, out) in enumerate(pairs):
        loads[k].wait()
        saves.append(pltpu.make_async_copy(held, out, save.at[k]))
        saves[-1].start()
    for copy in saves:
        copy.wait()


def emit_call(*results):
    return pl.pallas_call(
        emit_kernel,
        name="emit",
        out_shape=(
            shape((TOK, W * PIECES)), shape((1, W * PIECES), F32),
            shape((2 * W, W)), shape((W, 2 * W)),
        ),
        in_specs=[ANY, ANY, ANY, ANY],
        out_specs=(ANY, ANY, ANY, ANY),
        scratch_shapes=[
            pltpu.VMEM((WIDE, W), BF16), pltpu.VMEM((W, WIDE), BF16),
            pltpu.VMEM((TOK, W * PIECES), BF16), pltpu.VMEM((1, W * PIECES), F32),
            DMA((10,)), DMA((10,)),
        ],
    )(*results)


def per_device(features, delayed_error, ln_gain, w_in, w_out):
    results = block_call(features[0], delayed_error[0], ln_gain, w_in[0], w_out[0])
    passed, gain_grad, in_total, out_total = emit_call(*results)
    return passed[None], gain_grad, in_total[None], out_total[None]


def solution(mesh):
    return jax.shard_map(
        per_device,
        mesh=mesh,
        in_specs=(
            P("section", ("dp", "shard"), None),
            P("section", ("dp", "shard"), None),
            P("section", None),
            P("section", None, "shard"),
            P("section", "shard", None),
        ),
        out_specs=(
            P("section", ("dp", "shard"), None),
            P("section", None),
            P("section", "dp", "shard"),
            P("section", "shard", "dp"),
        ),
        check_vma=False,
    )
```

```python
import functools

import jax
import jax.numpy as jnp
from jax import lax
from jax.experimental import pallas as pl
from jax.experimental.pallas import tpu as pltpu
from jax.sharding import PartitionSpec as P

SQRT_HALF = 0.7071067811865476
INV_ROOT_TWO_PI = 0.3989422804014327
EPSILON = 1e-06
F32 = jnp.float32
BF16 = jnp.bfloat16
MESH = pl.DeviceIdType.MESH
W = 768
WIDE = 2 * W
HALF = 16
TOK = 32
GROUP = 512
PIECES = 8
ALL = 14
LIMIT = 66_900_000

def place():
    s = lax.axis_index("section")
    d = lax.axis_index("dp")
    j = lax.axis_index("shard")
    return s, d, j // 8, (j // 2) % 4, j % 2


def neighbour(dx=0, dh=0, dz=0, dc=0, ds=0):
    s, d, h, z, c = place()
    return (
        (s + ds) % 2,
        (d + dx + 4) % 4,
        ((h + dh) % 2) * 8 + ((z + dz + 4) % 4) * 2 + (c + dc) % 2,
    )


def greet(barrier, targets):
    for target in targets:
        pl.semaphore_signal(barrier, inc=1, device_id=target, device_id_type=MESH)
    pl.semaphore_wait(barrier, len(targets))


def dot(a, b, ca, cb):
    return lax.dot_general(
        a, b, (((ca,), (cb,)), ((), ())), preferred_element_type=F32
    )


FULL, LEFT, RIGHT = pl.ds(0, WIDE), pl.ds(0, W), pl.ds(W, W)


class Gather:
    def __init__(self, bufs, send, recv, core_recv):
        self.bufs, self.send, self.recv, self.core_recv = bufs, send, recv, core_recv

    def block(self, dh, dz, dc=0):
        _, _, h, z, c = place()
        index = ((h + dh) % 2) * 8 + ((z + dz + 4) % 4) * 2 + (c + dc) % 2
        return pl.ds(pl.multiple_of(index * HALF, HALF), HALF)

    def copy(self, p, a, rows, sem, target, source=None, cols=FULL):
        there = self.bufs[a].at[p, rows, cols]
        return pltpu.make_async_remote_copy(
            src_ref=there if source is None else source,
            dst_ref=there,
            send_sem=self.send.at[p],
            recv_sem=sem,
            device_id=target,
            device_id_type=MESH,
        )

    def put(self, stage, p, a, rows, target, source=None, cols=FULL):
        sem = self.recv.at[p, stage]
        self.copy(p, a, rows, sem, target, source, cols).start()

    def got(self, stage, p):
        rows = pl.ds(0, (6, 6, 2)[stage] * HALF)
        self.copy(p, 0, rows, self.recv.at[p, stage], neighbour(dz=1)).wait_recv()

    def to_core(self, p, a, dh, dz, source=None):
        sem = self.core_recv.at[p]
        self.copy(p, a, self.block(dh, dz), sem, neighbour(dc=1), source).start()

    def stage0(self, p, sources):
        up, down, across = neighbour(dz=1), neighbour(dz=-1), neighbour(dh=1)
        own = self.block(0, 0)
        for a in range(2):
            self.put(0, p, a, own, across, sources[a])
            self.put(0, p, a, own, up, sources[a])
            self.put(0, p, a, own, down, sources[a])
            self.to_core(p, a, 0, 0, sources[a])

    def stage1(self, p):
        up, down, across = neighbour(dz=1), neighbour(dz=-1), neighbour(dh=1)
        self.got(0, p)
        for a in range(2):
            if a == 0:
                self.put(1, p, 0, self.block(1, 0), up)
                self.put(1, p, 0, self.block(1, 0), down)
            else:
                self.put(1, p, 1, self.block(0, 1), across)
                self.put(1, p, 1, self.block(0, -1), across)
            self.put(1, p, a, self.block(0, 1), down, None, LEFT)
            self.put(1, p, a, self.block(0, -1), up, None, RIGHT)
            self.to_core(p, a, 1, 0)
            self.to_core(p, a, 0, 1)
            self.to_core(p, a, 0, -1)

    def stage2(self, p):
        up, down, across = neighbour(dz=1), neighbour(dz=-1), neighbour(dh=1)
        self.got(1, p)
        for a in range(2):
            if a == 0:
                self.put(2, p, 0, self.block(1, 1), down, None, LEFT)
                self.put(2, p, 0, self.block(1, -1), up, None, RIGHT)
            else:
                self.put(2, p, 1, self.block(0, 2), across)
            self.to_core(p, a, 1, 1)
            self.to_core(p, a, 1, -1)
            self.to_core(p, a, 0, 2)

    def stage3(self, p):
        self.got(2, p)
        for a in range(2):
            self.to_core(p, a, 1, 2)

    def stage4(self, p):
        rows = pl.ds(0, 16 * HALF)
        self.copy(p, 0, rows, self.core_recv.at[p], neighbour(dc=1)).wait_recv()

    def finish(self, p):
        part = self.bufs[0].at[pl.ds(0, 2), pl.ds(0, 15 * HALF), :]
        pltpu.make_async_copy(part, part, self.send.at[p]).wait()


def gather_scratch(pieces):
    return [
        pltpu.SemaphoreType.DMA((pieces,)),
        pltpu.SemaphoreType.DMA((pieces, 3)),
        pltpu.SemaphoreType.DMA((pieces,)),
    ]


def kernel(
    features, errors, gain, w_in, w_out,
    passed, gain_grad, in_grad, out_grad,
    all_normed, all_errors, acts, win, wout, part, paired, summed, hop1, hop2, total,
    last, in_acc, out_acc, normed, centred, inverses, norm_error, own_error,
    slice_normed, slice_errors, gains,
    send, recv, core_recv, c_send, c_recv, x_send, x_recv, w_sem,
    o_sem, rs_send, rs_recv, g_send, g_recv, p_send, p_recv,
):
    _, d, h, z, c = place()
    up, down, left, right = (
        neighbour(dz=1), neighbour(dz=-1), neighbour(dx=-1), neighbour(dx=1),
    )
    across, other, partner = neighbour(dh=1), neighbour(dc=1), neighbour(ds=1)

    def turn(p):
        return (p + d + 1) % 4

    def load_in(k):
        cols = pl.ds(pl.multiple_of(turn(k // 2) * WIDE + k % 2 * W, W), W)
        return pltpu.make_async_copy(
            w_in.at[cols, :], win.at[k % 3], w_sem.at[0, k % 3]
        )

    def load_out(k):
        cols = pl.ds(pl.multiple_of(turn(k // 2) * WIDE + k % 2 * W, W), W)
        return pltpu.make_async_copy(
            w_out.at[:, cols], wout.at[k % 2], w_sem.at[1, k % 2]
        )

    for k in range(3):
        load_in(k).start()
    for k in range(2):
        load_out(k).start()

    scale = gain[...]
    for first in range(0, TOK, 16):
        rows = pl.ds(first, 16)
        values = features[rows, :].astype(F32)
        average = jnp.mean(values, -1, keepdims=True)
        values = values - average
        variance = jnp.mean(values * values, -1, keepdims=True)
        inverse = lax.rsqrt(variance + EPSILON)
        values = values * inverse
        centred[rows, :] = values
        inverses[rows, :] = jnp.broadcast_to(inverse, (16, 128))
        normed[rows, :] = (values * scale).astype(BF16)

    gather = Gather((all_normed, all_errors), send, recv, core_recv)
    greet(
        pltpu.get_barrier_semaphore(),
        [up, down, left, right, across, other, partner]
        + [neighbour(dz=2), neighbour(dx=2), neighbour(dh=1, dc=1)],
    )

    def tokens(tau):
        return pl.ds(pl.multiple_of(tau * HALF, HALF), HALF)

    def crossing(g, tau, a):
        dx = (-1, 1, 2)[g]
        cols = pl.ds(pl.multiple_of((d + dx + 4) % 4 * WIDE, WIDE), WIDE)
        return pltpu.make_async_remote_copy(
            src_ref=(normed, errors)[a].at[tokens(tau), cols],
            dst_ref=(slice_normed, slice_errors)[a].at[tau * 3 + g],
            send_sem=c_send,
            recv_sem=c_recv.at[tau * 3 + g],
            device_id=neighbour(dx=dx),
            device_id_type=MESH,
        )

    def stage0(p):
        rows = tokens(p // 4)
        cols = pl.ds(pl.multiple_of(turn(p) * WIDE, WIDE), WIDE)
        gather.stage0(p, (normed.at[rows, cols], errors.at[rows, cols]))
        own = gather.block(0, 0)
        all_normed[p, own, :] = normed[rows, cols]
        all_errors[p, own, :] = errors[rows, cols]

    def stage0_slice(p):
        u = p - PIECES
        there = slice_normed.at[pl.ds(0, 2)]
        pltpu.make_async_copy(there, there, c_recv.at[u]).wait()
        gather.stage0(p, (slice_normed.at[u], slice_errors.at[u]))
        own = gather.block(0, 0)
        all_normed[p, own, :] = slice_normed[u]
        all_errors[p, own, :] = slice_errors[u]

    def hand(p, g, act):
        for buf in (all_normed, all_errors):
            for i in range(8):
                rows = pl.ds(pl.multiple_of((i * 2 + c) * HALF, HALF), HALF)
                act(
                    pltpu.make_async_remote_copy(
                        src_ref=buf.at[p, rows, :],
                        dst_ref=buf.at[PIECES + g, rows, :],
                        send_sem=send.at[PIECES + g],
                        recv_sem=recv.at[PIECES + g, 0],
                        device_id=(left, right)[g],
                        device_id_type=MESH,
                    )
                )

    def handed(g):
        there = all_normed.at[PIECES + g]
        pltpu.make_async_copy(there, there, recv.at[PIECES + g, 0]).wait()
        for buf in (all_normed, all_errors):
            for i in range(8):
                rows = pl.ds(pl.multiple_of((i * 2 + c) * HALF, HALF), HALF)
                pltpu.make_async_remote_copy(
                    src_ref=buf.at[PIECES + g, rows, :],
                    dst_ref=buf.at[PIECES + g, rows, :],
                    send_sem=send.at[PIECES + g],
                    recv_sem=core_recv.at[PIECES + g],
                    device_id=other,
                    device_id_type=MESH,
                ).start()

    def acting(tau):
        return pl.ds(pl.multiple_of(tau * 256, 256), 256)

    def activate(tau):
        @pl.loop(0, 8)
        def _(i):
            rows = pl.ds(pl.multiple_of(tau * 256 + i * 32, 32), 32)
            x = in_acc[0, rows, :]
            cdf = 0.5 * (1.0 + lax.erf(x * SQRT_HALF))
            density = INV_ROOT_TWO_PI * jnp.exp(-0.5 * x * x)
            acts[1, 3, rows, :] = (x * cdf).astype(BF16)
            acts[0, 3, rows, :] = (in_acc[1, rows, :] * (cdf + x * density)).astype(
                BF16
            )

    def sideways(tau, a, g, part_of):
        rows = pl.ds(pl.multiple_of(tau * 256 + part_of * 128, 128), 128)
        return pltpu.make_async_remote_copy(
            src_ref=acts.at[a, 3, rows, :],
            dst_ref=acts.at[a, g, rows, :],
            send_sem=x_send.at[tau],
            recv_sem=x_recv.at[tau, (part_of + g) % 2],
            device_id=(left, right)[g],
            device_id_type=MESH,
        )

    def onward(tau, a, g):
        rows = pl.ds(pl.multiple_of(tau * 256 + g * 128, 128), 128)
        return pltpu.make_async_remote_copy(
            src_ref=acts.at[a, g, rows, :],
            dst_ref=acts.at[a, 2, rows, :],
            send_sem=x_send.at[tau],
            recv_sem=x_recv.at[tau, 2],
            device_id=(left, right)[g],
            device_id_type=MESH,
        )

    def arrived(tau, k):
        there = acts.at[0, 0]
        pltpu.make_async_copy(there, there, x_recv.at[tau, k]).wait()

    def each(act):
        for a in range(2):
            for g in range(2):
                act(a, g)

    def move(k, q, source, target_ref, target):
        return pltpu.make_async_remote_copy(
            src_ref=source,
            dst_ref=target_ref,
            send_sem=rs_send.at[q, min(k, 1)],
            recv_sem=rs_recv.at[q, (k + 1) // 2],
            device_id=target,
            device_id_type=MESH,
        )

    zp, zm, zz = (z + 1) % 4, (z + 3) % 4, (z + 2) % 4

    def m0(q):
        return move(0, q, part.at[q % 3, :, :, 1 - c], paired.at[q], other)

    def m1(q):
        return move(1, q, summed.at[q, :, zz, :, LEFT], hop1.at[q, 0], up)

    def m2(q):
        return move(2, q, summed.at[q, :, zz, :, RIGHT], hop1.at[q, 1], down)

    def m3(q):
        return move(3, q, summed.at[q, :, zp], hop2.at[q, 0], up)

    def m4(q):
        return move(4, q, summed.at[q, :, zm], hop2.at[q, 1], down)

    def m5(q):
        return move(5, q, total.at[q, 1 - h], last.at[q], across)

    def scatter1(q):
        m0(q).wait_recv()
        for hh in range(2):
            for zi in range(4):
                summed[q, hh, zi] = (
                    part[q % 3, hh, zi, c].astype(F32) + paired[q, hh, zi].astype(F32)
                ).astype(BF16)
        m1(q).start()
        m2(q).start()

    def both(q, k, count):
        there = hop2.at[q, pl.ds(0, count)]
        pltpu.make_async_copy(there, there, rs_recv.at[q, k]).wait()

    def scatter2(q):
        both(q, 1, 1)
        for k, row, cols, go in ((0, zp, LEFT, m3), (1, zm, RIGHT, m4)):
            for hh in range(2):
                summed[q, hh, row, :, cols] = (
                    summed[q, hh, row, :, cols].astype(F32)
                    + hop1[q, k, hh].astype(F32)
                ).astype(BF16)
            go(q).start()

    def scatter3(q):
        both(q, 2, 2)
        for hh in range(2):
            total[q, hh] = (
                summed[q, hh, z].astype(F32)
                + hop2[q, 0, hh].astype(F32)
                + hop2[q, 1, hh].astype(F32)
            ).astype(BF16)
        m5(q).start()

    def scatter4(q):
        m5(q).wait_recv()
        cols = pl.ds(pl.multiple_of(turn(q) * WIDE, WIDE), WIDE)
        norm_error[tokens(q // 4), cols] = total[q, h].astype(F32) + last[q].astype(F32)

    def products(u, g, tau, half):
        cols = (LEFT, RIGHT)[half] if isinstance(half, int) else pl.ds(
            pl.multiple_of(half * W, W), W
        )
        rows = acting(tau)
        return (
            dot(all_normed[u, :, cols], acts[0, g, rows, :], 0, 0),
            dot(acts[1, g, rows, :], all_errors[u, :, cols], 0, 0),
        )

    def add_products(u, g, tau, half):
        to_in, to_out = products(u, g, tau, half)
        in_acc[half] += to_in
        out_acc[half] += to_out

    def correct(tau):
        rows = tokens(tau)
        scaled = norm_error[rows, :] * scale
        around = centred[rows, :]
        shift = jnp.mean(scaled, -1, keepdims=True)
        slope = jnp.mean(scaled * around, -1, keepdims=True)
        corrected = inverses[rows, pl.ds(0, 1)] * (scaled - shift - around * slope)
        own_error[rows, :] = (errors[rows, :].astype(F32) + corrected).astype(BF16)
        swap(tau).start()

    def swap(tau):
        return pltpu.make_async_remote_copy(
            src_ref=own_error.at[tokens(tau), :],
            dst_ref=passed.at[tokens(tau), :],
            send_sem=p_send.at[tau],
            recv_sem=p_recv.at[tau],
            device_id=partner,
            device_id_type=MESH,
        )

    def spread(level, k):
        target, slot = (
            ((neighbour(dc=1), neighbour(dh=1), neighbour(dh=1, dc=1))[k], h * 2 + c),
            (neighbour(dz=k + 1), z),
            (neighbour(dx=k + 1), d),
        )[level]
        return pltpu.make_async_remote_copy(
            src_ref=gains.at[level, slot],
            dst_ref=gains.at[level, slot],
            send_sem=g_send.at[level],
            recv_sem=g_recv.at[level],
            device_id=target,
            device_id_type=MESH,
        )

    def collect(level):
        there = gains.at[level, pl.ds(0, 3)]
        pltpu.make_async_copy(there, there, g_recv.at[level]).wait()
        value = gains[level, 0] + gains[level, 1] + gains[level, 2] + gains[level, 3]
        if level == 2:
            for q in range(PIECES):
                gain_grad[:, pl.ds(q * W, W)] = value[q : q + 1, :]
            return
        gains[level + 1, (z, d)[level]] = value
        for k in range(3):
            spread(level + 1, k).start()

    def start_gain():
        for q in range(PIECES):
            cols = pl.ds(q * W, W)
            product = norm_error[:, cols] * centred[:, cols]
            mine = jnp.sum(product, 0, keepdims=True)
            gains[0, h * 2 + c, pl.ds(q, 1), :] = mine
        for k in range(3):
            spread(0, k).start()

    @pl.loop(0, 20)
    def _(t):
        @pl.when((t == 8) | (t == 12))
        def _():
            tau = t // 4 - 2
            activate(tau)
            each(lambda a, g: sideways(tau, a, g, g).start())
            each(lambda a, g: sideways(tau, a, g, 1 - g).start())

        @pl.when(t < PIECES)
        def _():
            stage0(t)

        @pl.when(t == 0)
        def _():
            for tau, g in ((0, 2), (1, 0), (1, 1), (1, 2)):
                for a in range(2):
                    crossing(g, tau, a).start()

        @pl.when((t >= 1) & (t < PIECES + 1))
        def _():
            gather.stage1(t - 1)

        @pl.when((t >= 2) & (t < PIECES + 2))
        def _():
            gather.stage2(t - 2)

        @pl.when((t >= 3) & (t < PIECES + 3))
        def _():
            gather.stage3(t - 3)

        @pl.when((t >= 4) & (t < PIECES + 4))
        def _():
            gather.stage4(t - 4)

        @pl.when(t == 4)
        def _():
            hand(0, 1, lambda copy: copy.start())

        @pl.when(t == 6)
        def _():
            hand(2, 0, lambda copy: copy.start())

        @pl.when(t >= 11)
        def _():
            @pl.when(t < 16)
            def _():
                m0(t - 11).wait_send()

        @pl.when((t >= 4) & (t < 16))
        def _():
            @pl.loop(0, 2)
            def _(half):
                k = (t - 4) * 2 + half
                cols = pl.ds(pl.multiple_of(half * W, W), W)
                load_in(k).wait()

                @pl.when(t < PIECES + 4)
                def _():
                    p = t - 4
                    load_out(k).wait()
                    pre = dot(all_normed[p, :, cols], win[k % 3], 1, 0)
                    back = dot(all_errors[p, :, cols], wout[k % 2], 1, 1)
                    rows = acting(p // 4)

                    @pl.when(k % 8 == 0)
                    def _():
                        in_acc[0, rows, :] = pre
                        in_acc[1, rows, :] = back

                    @pl.when(k % 8 > 0)
                    def _():
                        in_acc[0, rows, :] += pre
                        in_acc[1, rows, :] += back

                    @pl.when(k < 14)
                    def _():
                        load_out(k + 2).start()

                @pl.when(t >= 8)
                def _():
                    q = t - 8
                    known = acts[0, 3, acting(q // 4), :]
                    value = dot(known, win[k % 3], 1, 1).astype(BF16)
                    part[q % 3, :, :, :, :, cols] = value.reshape(2, 4, 2, HALF, W)

                @pl.when(k < 21)
                def _():
                    load_in(k + 3).start()

            @pl.when(t >= 8)
            def _():
                m0(t - 8).start()

        @pl.when((t >= 9) & (t < 17))
        def _():
            scatter1(t - 9)

        @pl.when((t >= 10) & (t < 18))
        def _():
            scatter2(t - 10)

        @pl.when((t >= 11) & (t < 19))
        def _():
            scatter3(t - 11)

        @pl.when((t >= 12) & (t < 20))
        def _():
            scatter4(t - 12)

        @pl.when((t == 9) | ((t >= 13) & (t < 16)))
        def _():
            stage0_slice(t + 1 - 3 * (t // 13))

        @pl.when((t == 10) | ((t >= 15) & (t < 18)))
        def _():
            gather.stage1(t - 4 * (t // 15))

        @pl.when((t == 11) | ((t >= 16) & (t < 19)))
        def _():
            gather.stage2(t - 1 - 4 * (t // 16))

        @pl.when((t == 12) | (t >= 17))
        def _():
            gather.stage3(t - 2 - 4 * (t // 17))

        @pl.when(t == 10)
        def _():
            handed(1)

        @pl.when(t == 12)
        def _():
            handed(0)

        @pl.when((t == 11) | (t == 15))
        def _():
            tau = (t - 11) // 4
            arrived(tau, 0)
            each(lambda a, g: onward(tau, a, g).start())

        @pl.when(t == 14)
        def _():
            arrived(0, 1)

        @pl.when(t == 16)
        def _():
            correct(0)

        @pl.when(t == 17)
        def _():
            arrived(0, 2)

        @pl.when((t == 12) | (t == 13))
        def _():
            tau = t - 12

            @pl.loop(0, 2)
            def _(half):
                to_in, to_out = products(tau * 4 + 3, 3, tau, half)

                @pl.when(tau == 0)
                def _():
                    in_acc[half] = to_in
                    out_acc[half] = to_out

                @pl.when(tau == 1)
                def _():
                    in_acc[half] += to_in
                    out_acc[half] += to_out

        @pl.when(t == 19)
        def _():
            start_gain()
            correct(1)

        @pl.when((t >= 15) & (t < 18))
        def _():
            u = t - 15
            gather.stage4(PIECES + u)

            @pl.loop(0, 2)
            def _(half):
                add_products(PIECES + u, u % 3, u // 3, half)

    arrived(1, 1)

    @pl.loop(3, 5)
    def _(u):
        gather.stage4(PIECES + u)

        @pl.loop(0, 2)
        def _(half):
            add_products(PIECES + u, u - 3, 1, half)

        @pl.when(u == 3)
        def _():
            collect(0)

        @pl.when(u == 4)
        def _():
            collect(1)

    arrived(1, 2)
    gather.stage4(13)

    def emit(half):
        part_of = pl.ds(pl.multiple_of(half * W, W), W)
        return (
            pltpu.make_async_copy(win.at[0], in_grad.at[part_of, :], o_sem.at[0]),
            pltpu.make_async_copy(win.at[1], out_grad.at[:, part_of], o_sem.at[1]),
        )

    @pl.loop(0, 2)
    def _(half):
        add_products(13, 2, 1, half)

        @pl.when(half == 1)
        def _():
            for copy in emit(0):
                copy.wait()

        win[0] = in_acc[half].astype(BF16)
        win[1] = out_acc[half].astype(BF16)
        for copy in emit(half):
            copy.start()

    part_of = all_normed.at[0, pl.ds(0, 8 * HALF), :]
    pltpu.make_async_copy(part_of, part_of, c_send).wait()
    for tau in range(2):
        part_of = acts.at[0, pl.ds(0, 3)]
        pltpu.make_async_copy(part_of, part_of, x_send.at[tau]).wait()

    @pl.loop(0, ALL)
    def _(p):
        @pl.when((p < PIECES) | (p >= PIECES + 2))
        def _():
            gather.finish(p)

        @pl.when((p >= PIECES) & (p < PIECES + 2))
        def _():
            there = all_normed.at[pl.ds(0, 2)]
            pltpu.make_async_copy(there, there, send.at[p]).wait()

    @pl.loop(0, PIECES)
    def _(q):
        @pl.when(q >= 5)
        def _():
            m0(q).wait_send()

        part_of = all_normed.at[0, pl.ds(0, 7 * HALF), :]
        pltpu.make_async_copy(part_of, part_of, rs_send.at[q, 1]).wait()

    collect(2)
    for level in range(3):
        there = gains.at[level, pl.ds(0, 3)]
        pltpu.make_async_copy(there, there, g_send.at[level]).wait()
    for tau in range(2):
        swap(tau).wait()
    for copy in emit(1):
        copy.wait()


def shape(dims, dtype=BF16):
    return jax.ShapeDtypeStruct(dims, dtype)


VM = pl.BlockSpec(memory_space=pltpu.VMEM)
ANY = pl.BlockSpec(memory_space=pl.ANY)
DMA = pltpu.SemaphoreType.DMA


def block_call(features, errors, gain, w_in, w_out):
    bf16, f32 = functools.partial(pltpu.VMEM, dtype=BF16), functools.partial(
        pltpu.VMEM, dtype=F32
    )
    return pl.pallas_call(
        kernel,
        name="block",
        out_shape=(
            shape((TOK, W * PIECES)), shape((1, W * PIECES), F32),
            shape((2 * W, W)), shape((W, 2 * W)),
        ),
        in_specs=[VM, VM, VM, ANY, ANY],
        out_specs=(ANY, VM, ANY, ANY),
        scratch_shapes=[
            bf16((ALL, 16 * HALF, WIDE)),
            bf16((ALL, 16 * HALF, WIDE)),
            bf16((2, 4, GROUP, W)),
            bf16((3, W, W)),
            bf16((2, W, W)),
            bf16((3, 2, 4, 2, HALF, WIDE)),
            bf16((PIECES, 2, 4, HALF, WIDE)),
            bf16((PIECES, 2, 4, HALF, WIDE)),
            bf16((PIECES, 2, 2, HALF, W)),
            bf16((PIECES, 2, 2, HALF, WIDE)),
            bf16((PIECES, 2, HALF, WIDE)),
            bf16((PIECES, HALF, WIDE)),
            f32((2, W, W)),
            f32((2, W, W)),
            bf16((TOK, W * PIECES)),
            f32((TOK, W * PIECES)),
            f32((TOK, 128)),
            f32((TOK, W * PIECES)),
            bf16((TOK, W * PIECES)),
            bf16((6, HALF, WIDE)),
            bf16((6, HALF, WIDE)),
            f32((3, 4, 8, W)),
            *gather_scratch(ALL),
            DMA, DMA((6,)), DMA((2,)), DMA((2, 3)), DMA((2, 3)), DMA((2,)),
            DMA((PIECES, 2)), DMA((PIECES, 4)), DMA((3,)), DMA((3,)),
            DMA((2,)), DMA((2,)),
        ],
        compiler_params=pltpu.CompilerParams(
            collective_id=0, has_side_effects=True, vmem_limit_bytes=LIMIT
        ),
    )(features, errors, gain, w_in, w_out)


def emit_kernel(
    passed, gain, in_grad, out_grad,
    passed_out, gain_out, in_out, out_out,
    a, b, held_passed, held_gain, load, save,
):
    pairs = []
    for k in range(4):
        rows = pl.ds(k * 384, 384)
        pairs.append((in_grad.at[rows, :], a.at[rows, :], in_out.at[rows, :]))
        rows = pl.ds(k * 192, 192)
        pairs.append((out_grad.at[rows, :], b.at[rows, :], out_out.at[rows, :]))
    pairs.append((passed, held_passed, passed_out))
    pairs.append((gain, held_gain, gain_out))
    loads = [
        pltpu.make_async_copy(source, held, load.at[k])
        for k, (source, held, _) in enumerate(pairs)
    ]
    for copy in loads:
        copy.start()
    saves = []
    for k, (_, held, out) in enumerate(pairs):
        loads[k].wait()
        saves.append(pltpu.make_async_copy(held, out, save.at[k]))
        saves[-1].start()
    for copy in saves:
        copy.wait()


def emit_call(*results):
    return pl.pallas_call(
        emit_kernel,
        name="emit",
        out_shape=(
            shape((TOK, W * PIECES)), shape((1, W * PIECES), F32),
            shape((2 * W, W)), shape((W, 2 * W)),
        ),
        in_specs=[ANY, ANY, ANY, ANY],
        out_specs=(ANY, ANY, ANY, ANY),
        scratch_shapes=[
            pltpu.VMEM((WIDE, W), BF16), pltpu.VMEM((W, WIDE), BF16),
            pltpu.VMEM((TOK, W * PIECES), BF16), pltpu.VMEM((1, W * PIECES), F32),
            DMA((10,)), DMA((10,)),
        ],
    )(*results)


def per_device(features, delayed_error, ln_gain, w_in, w_out):
    results = block_call(features[0], delayed_error[0], ln_gain, w_in[0], w_out[0])
    passed, gain_grad, in_total, out_total = emit_call(*results)
    return passed[None], gain_grad, in_total[None], out_total[None]


def solution(mesh):
    return jax.shard_map(
        per_device,
        mesh=mesh,
        in_specs=(
            P("section", ("dp", "shard"), None),
            P("section", ("dp", "shard"), None),
            P("section", None),
            P("section", None, "shard"),
            P("section", "shard", None),
        ),
        out_specs=(
            P("section", ("dp", "shard"), None),
            P("section", None),
            P("section", "dp", "shard"),
            P("section", "shard", "dp"),
        ),
        check_vma=False,
    )
```

```python
import functools

import jax
import jax.numpy as jnp
from jax import lax
from jax.experimental import pallas as pl
from jax.experimental.pallas import tpu as pltpu
from jax.sharding import PartitionSpec as P

SQRT_HALF = 0.7071067811865476
INV_ROOT_TWO_PI = 0.3989422804014327
EPSILON = 1e-06
F32 = jnp.float32
BF16 = jnp.bfloat16
MESH = pl.DeviceIdType.MESH
W = 768
WIDE = 2 * W
HALF = 16
TOK = 32
GROUP = 512
PIECES = 8
ALL = 14
LIMIT = 66_900_000

def place():
    s = lax.axis_index("section")
    d = lax.axis_index("dp")
    j = lax.axis_index("shard")
    return s, d, j // 8, (j // 2) % 4, j % 2


def neighbour(dx=0, dh=0, dz=0, dc=0, ds=0):
    s, d, h, z, c = place()
    return (
        (s + ds) % 2,
        (d + dx + 4) % 4,
        ((h + dh) % 2) * 8 + ((z + dz + 4) % 4) * 2 + (c + dc) % 2,
    )


def greet(barrier, targets):
    for target in targets:
        pl.semaphore_signal(barrier, inc=1, device_id=target, device_id_type=MESH)
    pl.semaphore_wait(barrier, len(targets))


def dot(a, b, ca, cb):
    return lax.dot_general(
        a, b, (((ca,), (cb,)), ((), ())), preferred_element_type=F32
    )


FULL, LEFT, RIGHT = pl.ds(0, WIDE), pl.ds(0, W), pl.ds(W, W)


class Gather:
    def __init__(self, bufs, send, recv, core_recv):
        self.bufs, self.send, self.recv, self.core_recv = bufs, send, recv, core_recv

    def block(self, dh, dz, dc=0):
        _, _, h, z, c = place()
        index = ((h + dh) % 2) * 8 + ((z + dz + 4) % 4) * 2 + (c + dc) % 2
        return pl.ds(pl.multiple_of(index * HALF, HALF), HALF)

    def copy(self, p, a, rows, sem, target, source=None, cols=FULL):
        there = self.bufs[a].at[p, rows, cols]
        return pltpu.make_async_remote_copy(
            src_ref=there if source is None else source,
            dst_ref=there,
            send_sem=self.send.at[p],
            recv_sem=sem,
            device_id=target,
            device_id_type=MESH,
        )

    def put(self, stage, p, a, rows, target, source=None, cols=FULL):
        sem = self.recv.at[p, stage]
        self.copy(p, a, rows, sem, target, source, cols).start()

    def got(self, stage, p):
        rows = pl.ds(0, (6, 6, 2)[stage] * HALF)
        self.copy(p, 0, rows, self.recv.at[p, stage], neighbour(dz=1)).wait_recv()

    def to_core(self, p, a, dh, dz, source=None):
        sem = self.core_recv.at[p]
        self.copy(p, a, self.block(dh, dz), sem, neighbour(dc=1), source).start()

    def stage0(self, p, sources):
        up, down, across = neighbour(dz=1), neighbour(dz=-1), neighbour(dh=1)
        own = self.block(0, 0)
        for a in range(2):
            self.put(0, p, a, own, across, sources[a])
            self.put(0, p, a, own, up, sources[a])
            self.put(0, p, a, own, down, sources[a])
            self.to_core(p, a, 0, 0, sources[a])

    def stage1(self, p):
        up, down, across = neighbour(dz=1), neighbour(dz=-1), neighbour(dh=1)
        self.got(0, p)
        for a in range(2):
            if a == 0:
                self.put(1, p, 0, self.block(1, 0), up)
                self.put(1, p, 0, self.block(1, 0), down)
            else:
                self.put(1, p, 1, self.block(0, 1), across)
                self.put(1, p, 1, self.block(0, -1), across)
            self.put(1, p, a, self.block(0, 1), down, None, LEFT)
            self.put(1, p, a, self.block(0, -1), up, None, RIGHT)
            self.to_core(p, a, 1, 0)
            self.to_core(p, a, 0, 1)
            self.to_core(p, a, 0, -1)

    def stage2(self, p):
        up, down, across = neighbour(dz=1), neighbour(dz=-1), neighbour(dh=1)
        self.got(1, p)
        for a in range(2):
            if a == 0:
                self.put(2, p, 0, self.block(1, 1), down, None, LEFT)
                self.put(2, p, 0, self.block(1, -1), up, None, RIGHT)
            else:
                self.put(2, p, 1, self.block(0, 2), across)
            self.to_core(p, a, 1, 1)
            self.to_core(p, a, 1, -1)
            self.to_core(p, a, 0, 2)

    def stage3(self, p):
        self.got(2, p)
        for a in range(2):
            self.to_core(p, a, 1, 2)

    def stage4(self, p):
        rows = pl.ds(0, 16 * HALF)
        self.copy(p, 0, rows, self.core_recv.at[p], neighbour(dc=1)).wait_recv()

    def finish(self, p):
        part = self.bufs[0].at[pl.ds(0, 2), pl.ds(0, 15 * HALF), :]
        pltpu.make_async_copy(part, part, self.send.at[p]).wait()


def gather_scratch(pieces):
    return [
        pltpu.SemaphoreType.DMA((pieces,)),
        pltpu.SemaphoreType.DMA((pieces, 3)),
        pltpu.SemaphoreType.DMA((pieces,)),
    ]


def kernel(
    features, errors, gain, w_in, w_out,
    passed, gain_grad, in_grad, out_grad,
    all_normed, all_errors, acts, win, wout, part, paired, summed, hop1, hop2, total,
    last, in_acc, out_acc, normed, centred, inverses, norm_error, own_error,
    slice_normed, slice_errors, gains,
    send, recv, core_recv, c_send, c_recv, x_send, x_recv, w_sem,
    o_sem, rs_send, rs_recv, g_send, g_recv, p_send, p_recv,
):
    _, d, h, z, c = place()
    up, down, left, right = (
        neighbour(dz=1), neighbour(dz=-1), neighbour(dx=-1), neighbour(dx=1),
    )
    across, other, partner = neighbour(dh=1), neighbour(dc=1), neighbour(ds=1)

    def turn(p):
        return (p + d + 1) % 4

    def load_in(k):
        cols = pl.ds(pl.multiple_of(turn(k // 2) * WIDE + k % 2 * W, W), W)
        return pltpu.make_async_copy(
            w_in.at[cols, :], win.at[k % 3], w_sem.at[0, k % 3]
        )

    def load_out(k):
        cols = pl.ds(pl.multiple_of(turn(k // 2) * WIDE + k % 2 * W, W), W)
        return pltpu.make_async_copy(
            w_out.at[:, cols], wout.at[k % 2], w_sem.at[1, k % 2]
        )

    for k in range(3):
        load_in(k).start()
    for k in range(2):
        load_out(k).start()

    scale = gain[...]
    for first in range(0, TOK, 16):
        rows = pl.ds(first, 16)
        values = features[rows, :].astype(F32)
        average = jnp.mean(values, -1, keepdims=True)
        values = values - average
        variance = jnp.mean(values * values, -1, keepdims=True)
        inverse = lax.rsqrt(variance + EPSILON)
        values = values * inverse
        centred[rows, :] = values
        inverses[rows, :] = jnp.broadcast_to(inverse, (16, 128))
        normed[rows, :] = (values * scale).astype(BF16)

    gather = Gather((all_normed, all_errors), send, recv, core_recv)
    greet(
        pltpu.get_barrier_semaphore(),
        [up, down, left, right, across, other, partner]
        + [neighbour(dz=2), neighbour(dx=2), neighbour(dh=1, dc=1)],
    )

    def tokens(tau):
        return pl.ds(pl.multiple_of(tau * HALF, HALF), HALF)

    def crossing(g, tau, a):
        dx = (-1, 1, 2)[g]
        cols = pl.ds(pl.multiple_of((d + dx + 4) % 4 * WIDE, WIDE), WIDE)
        return pltpu.make_async_remote_copy(
            src_ref=(normed, errors)[a].at[tokens(tau), cols],
            dst_ref=(slice_normed, slice_errors)[a].at[tau * 3 + g],
            send_sem=c_send,
            recv_sem=c_recv.at[tau * 3 + g],
            device_id=neighbour(dx=dx),
            device_id_type=MESH,
        )

    def stage0(p):
        rows = tokens(p // 4)
        cols = pl.ds(pl.multiple_of(turn(p) * WIDE, WIDE), WIDE)
        gather.stage0(p, (normed.at[rows, cols], errors.at[rows, cols]))
        own = gather.block(0, 0)
        all_normed[p, own, :] = normed[rows, cols]
        all_errors[p, own, :] = errors[rows, cols]

    def stage0_slice(p):
        u = p - PIECES
        there = slice_normed.at[pl.ds(0, 2)]
        pltpu.make_async_copy(there, there, c_recv.at[u]).wait()
        gather.stage0(p, (slice_normed.at[u], slice_errors.at[u]))
        own = gather.block(0, 0)
        all_normed[p, own, :] = slice_normed[u]
        all_errors[p, own, :] = slice_errors[u]

    def hand(p, g, act):
        for buf in (all_normed, all_errors):
            for i in range(8):
                rows = pl.ds(pl.multiple_of((i * 2 + c) * HALF, HALF), HALF)
                act(
                    pltpu.make_async_remote_copy(
                        src_ref=buf.at[p, rows, :],
                        dst_ref=buf.at[PIECES + g, rows, :],
                        send_sem=send.at[PIECES + g],
                        recv_sem=recv.at[PIECES + g, 0],
                        device_id=(left, right)[g],
                        device_id_type=MESH,
                    )
                )

    def handed(g):
        there = all_normed.at[PIECES + g]
        pltpu.make_async_copy(there, there, recv.at[PIECES + g, 0]).wait()
        for buf in (all_normed, all_errors):
            for i in range(8):
                rows = pl.ds(pl.multiple_of((i * 2 + c) * HALF, HALF), HALF)
                pltpu.make_async_remote_copy(
                    src_ref=buf.at[PIECES + g, rows, :],
                    dst_ref=buf.at[PIECES + g, rows, :],
                    send_sem=send.at[PIECES + g],
                    recv_sem=core_recv.at[PIECES + g],
                    device_id=other,
                    device_id_type=MESH,
                ).start()

    def acting(tau):
        return pl.ds(pl.multiple_of(tau * 256, 256), 256)

    def activate(tau):
        @pl.loop(0, 8)
        def _(i):
            rows = pl.ds(pl.multiple_of(tau * 256 + i * 32, 32), 32)
            x = in_acc[0, rows, :]
            cdf = 0.5 * (1.0 + lax.erf(x * SQRT_HALF))
            density = INV_ROOT_TWO_PI * jnp.exp(-0.5 * x * x)
            acts[1, 3, rows, :] = (x * cdf).astype(BF16)
            acts[0, 3, rows, :] = (in_acc[1, rows, :] * (cdf + x * density)).astype(
                BF16
            )

    def sideways(tau, a, g, part_of):
        rows = pl.ds(pl.multiple_of(tau * 256 + part_of * 128, 128), 128)
        return pltpu.make_async_remote_copy(
            src_ref=acts.at[a, 3, rows, :],
            dst_ref=acts.at[a, g, rows, :],
            send_sem=x_send.at[tau],
            recv_sem=x_recv.at[tau, (part_of + g) % 2],
            device_id=(left, right)[g],
            device_id_type=MESH,
        )

    def onward(tau, a, g):
        rows = pl.ds(pl.multiple_of(tau * 256 + g * 128, 128), 128)
        return pltpu.make_async_remote_copy(
            src_ref=acts.at[a, g, rows, :],
            dst_ref=acts.at[a, 2, rows, :],
            send_sem=x_send.at[tau],
            recv_sem=x_recv.at[tau, 2],
            device_id=(left, right)[g],
            device_id_type=MESH,
        )

    def arrived(tau, k):
        there = acts.at[0, 0]
        pltpu.make_async_copy(there, there, x_recv.at[tau, k]).wait()

    def each(act):
        for a in range(2):
            for g in range(2):
                act(a, g)

    def move(k, q, source, target_ref, target):
        return pltpu.make_async_remote_copy(
            src_ref=source,
            dst_ref=target_ref,
            send_sem=rs_send.at[q, min(k, 1)],
            recv_sem=rs_recv.at[q, (k + 1) // 2],
            device_id=target,
            device_id_type=MESH,
        )

    zp, zm, zz = (z + 1) % 4, (z + 3) % 4, (z + 2) % 4

    def m0(q):
        return move(0, q, part.at[q % 3, :, :, 1 - c], paired.at[q], other)

    def m1(q):
        return move(1, q, summed.at[q, :, zz, :, LEFT], hop1.at[q, 0], up)

    def m2(q):
        return move(2, q, summed.at[q, :, zz, :, RIGHT], hop1.at[q, 1], down)

    def m3(q):
        return move(3, q, summed.at[q, :, zp], hop2.at[q, 0], up)

    def m4(q):
        return move(4, q, summed.at[q, :, zm], hop2.at[q, 1], down)

    def m5(q):
        return move(5, q, total.at[q, 1 - h], last.at[q], across)

    def scatter1(q):
        m0(q).wait_recv()
        for hh in range(2):
            for zi in range(4):
                summed[q, hh, zi] = (
                    part[q % 3, hh, zi, c].astype(F32) + paired[q, hh, zi].astype(F32)
                ).astype(BF16)
        m1(q).start()
        m2(q).start()

    def both(q, k, count):
        there = hop2.at[q, pl.ds(0, count)]
        pltpu.make_async_copy(there, there, rs_recv.at[q, k]).wait()

    def scatter2(q):
        both(q, 1, 1)
        for k, row, cols, go in ((0, zp, LEFT, m3), (1, zm, RIGHT, m4)):
            for hh in range(2):
                summed[q, hh, row, :, cols] = (
                    summed[q, hh, row, :, cols].astype(F32)
                    + hop1[q, k, hh].astype(F32)
                ).astype(BF16)
            go(q).start()

    def scatter3(q):
        both(q, 2, 2)
        for hh in range(2):
            total[q, hh] = (
                summed[q, hh, z].astype(F32)
                + hop2[q, 0, hh].astype(F32)
                + hop2[q, 1, hh].astype(F32)
            ).astype(BF16)
        m5(q).start()

    def scatter4(q):
        m5(q).wait_recv()
        cols = pl.ds(pl.multiple_of(turn(q) * WIDE, WIDE), WIDE)
        norm_error[tokens(q // 4), cols] = total[q, h].astype(F32) + last[q].astype(F32)

    def products(u, g, tau, half):
        cols = (LEFT, RIGHT)[half] if isinstance(half, int) else pl.ds(
            pl.multiple_of(half * W, W), W
        )
        rows = acting(tau)
        return (
            dot(all_normed[u, :, cols], acts[0, g, rows, :], 0, 0),
            dot(acts[1, g, rows, :], all_errors[u, :, cols], 0, 0),
        )

    def add_products(u, g, tau, half):
        to_in, to_out = products(u, g, tau, half)
        in_acc[half] += to_in
        out_acc[half] += to_out

    def correct(tau):
        rows = tokens(tau)
        scaled = norm_error[rows, :] * scale
        around = centred[rows, :]
        shift = jnp.mean(scaled, -1, keepdims=True)
        slope = jnp.mean(scaled * around, -1, keepdims=True)
        corrected = inverses[rows, pl.ds(0, 1)] * (scaled - shift - around * slope)
        own_error[rows, :] = (errors[rows, :].astype(F32) + corrected).astype(BF16)
        swap(tau).start()

    def swap(tau):
        return pltpu.make_async_remote_copy(
            src_ref=own_error.at[tokens(tau), :],
            dst_ref=passed.at[tokens(tau), :],
            send_sem=p_send.at[tau],
            recv_sem=p_recv.at[tau],
            device_id=partner,
            device_id_type=MESH,
        )

    def spread(level, k):
        target, slot = (
            ((neighbour(dc=1), neighbour(dh=1), neighbour(dh=1, dc=1))[k], h * 2 + c),
            (neighbour(dz=k + 1), z),
            (neighbour(dx=k + 1), d),
        )[level]
        return pltpu.make_async_remote_copy(
            src_ref=gains.at[level, slot],
            dst_ref=gains.at[level, slot],
            send_sem=g_send.at[level],
            recv_sem=g_recv.at[level],
            device_id=target,
            device_id_type=MESH,
        )

    def collect(level):
        there = gains.at[level, pl.ds(0, 3)]
        pltpu.make_async_copy(there, there, g_recv.at[level]).wait()
        value = gains[level, 0] + gains[level, 1] + gains[level, 2] + gains[level, 3]
        if level == 2:
            for q in range(PIECES):
                gain_grad[:, pl.ds(q * W, W)] = value[q : q + 1, :]
            return
        gains[level + 1, (z, d)[level]] = value
        for k in range(3):
            spread(level + 1, k).start()

    def start_gain():
        for q in range(PIECES):
            cols = pl.ds(q * W, W)
            product = norm_error[:, cols] * centred[:, cols]
            mine = jnp.sum(product, 0, keepdims=True)
            gains[0, h * 2 + c, pl.ds(q, 1), :] = mine
        for k in range(3):
            spread(0, k).start()

    @pl.loop(0, 20)
    def _(t):
        @pl.when((t == 8) | (t == 12))
        def _():
            tau = t // 4 - 2
            activate(tau)
            each(lambda a, g: sideways(tau, a, g, g).start())
            each(lambda a, g: sideways(tau, a, g, 1 - g).start())

        @pl.when(t < PIECES)
        def _():
            stage0(t)

        @pl.when(t == 0)
        def _():
            for tau, g in ((0, 2), (1, 0), (1, 1), (1, 2)):
                for a in range(2):
                    crossing(g, tau, a).start()

        @pl.when((t >= 1) & (t < PIECES + 1))
        def _():
            gather.stage1(t - 1)

        @pl.when((t >= 2) & (t < PIECES + 2))
        def _():
            gather.stage2(t - 2)

        @pl.when((t >= 3) & (t < PIECES + 3))
        def _():
            gather.stage3(t - 3)

        @pl.when((t >= 4) & (t < PIECES + 4))
        def _():
            gather.stage4(t - 4)

        @pl.when(t == 4)
        def _():
            hand(0, 1, lambda copy: copy.start())

        @pl.when(t == 6)
        def _():
            hand(2, 0, lambda copy: copy.start())

        @pl.when(t >= 11)
        def _():
            @pl.when(t < 16)
            def _():
                m0(t - 11).wait_send()

        @pl.when((t >= 4) & (t < 16))
        def _():
            @pl.loop(0, 2)
            def _(half):
                k = (t - 4) * 2 + half
                cols = pl.ds(pl.multiple_of(half * W, W), W)
                load_in(k).wait()

                @pl.when(t < PIECES + 4)
                def _():
                    p = t - 4
                    load_out(k).wait()
                    pre = dot(all_normed[p, :, cols], win[k % 3], 1, 0)
                    back = dot(all_errors[p, :, cols], wout[k % 2], 1, 1)
                    rows = acting(p // 4)

                    @pl.when(k % 8 == 0)
                    def _():
                        in_acc[0, rows, :] = pre
                        in_acc[1, rows, :] = back

                    @pl.when(k % 8 > 0)
                    def _():
                        in_acc[0, rows, :] += pre
                        in_acc[1, rows, :] += back

                    @pl.when(k < 14)
                    def _():
                        load_out(k + 2).start()

                @pl.when(t >= 8)
                def _():
                    q = t - 8
                    known = acts[0, 3, acting(q // 4), :]
                    value = dot(known, win[k % 3], 1, 1).astype(BF16)
                    part[q % 3, :, :, :, :, cols] = value.reshape(2, 4, 2, HALF, W)

                @pl.when(k < 21)
                def _():
                    load_in(k + 3).start()

            @pl.when(t >= 8)
            def _():
                m0(t - 8).start()

        @pl.when((t >= 9) & (t < 17))
        def _():
            scatter1(t - 9)

        @pl.when((t >= 10) & (t < 18))
        def _():
            scatter2(t - 10)

        @pl.when((t >= 11) & (t < 19))
        def _():
            scatter3(t - 11)

        @pl.when((t >= 12) & (t < 20))
        def _():
            scatter4(t - 12)

        @pl.when((t == 9) | ((t >= 12) & (t < 15)))
        def _():
            stage0_slice(t + 1 - 2 * (t // 12))

        @pl.when((t == 10) | ((t >= 14) & (t < 17)))
        def _():
            gather.stage1(t - 3 * (t // 14))

        @pl.when((t == 11) | ((t >= 15) & (t < 18)))
        def _():
            gather.stage2(t - 1 - 3 * (t // 15))

        @pl.when((t == 12) | ((t >= 16) & (t < 19)))
        def _():
            gather.stage3(t - 2 - 3 * (t // 16))

        @pl.when(t == 10)
        def _():
            handed(1)

        @pl.when(t == 12)
        def _():
            handed(0)

        @pl.when((t == 11) | (t == 15))
        def _():
            tau = (t - 11) // 4
            arrived(tau, 0)
            each(lambda a, g: onward(tau, a, g).start())

        @pl.when(t == 14)
        def _():
            arrived(0, 1)

        @pl.when(t == 16)
        def _():
            correct(0)

        @pl.when(t == 17)
        def _():
            arrived(0, 2)

        @pl.when((t == 12) | (t == 13))
        def _():
            tau = t - 12

            @pl.loop(0, 2)
            def _(half):
                to_in, to_out = products(tau * 4 + 3, 3, tau, half)

                @pl.when(tau == 0)
                def _():
                    in_acc[half] = to_in
                    out_acc[half] = to_out

                @pl.when(tau == 1)
                def _():
                    in_acc[half] += to_in
                    out_acc[half] += to_out

        @pl.when(t == 19)
        def _():
            start_gain()
            correct(1)

        @pl.when((t >= 15) & (t < 18))
        def _():
            u = t - 15
            gather.stage4(PIECES + u)

            @pl.loop(0, 2)
            def _(half):
                add_products(PIECES + u, u % 3, u // 3, half)

    arrived(1, 1)

    @pl.loop(3, 5)
    def _(u):
        gather.stage4(PIECES + u)

        @pl.loop(0, 2)
        def _(half):
            add_products(PIECES + u, u - 3, 1, half)

        @pl.when(u == 3)
        def _():
            collect(0)

        @pl.when(u == 4)
        def _():
            collect(1)

    arrived(1, 2)
    gather.stage4(13)

    def emit(half):
        part_of = pl.ds(pl.multiple_of(half * W, W), W)
        return (
            pltpu.make_async_copy(win.at[0], in_grad.at[part_of, :], o_sem.at[0]),
            pltpu.make_async_copy(win.at[1], out_grad.at[:, part_of], o_sem.at[1]),
        )

    @pl.loop(0, 2)
    def _(half):
        add_products(13, 2, 1, half)

        @pl.when(half == 1)
        def _():
            for copy in emit(0):
                copy.wait()

        win[0] = in_acc[half].astype(BF16)
        win[1] = out_acc[half].astype(BF16)
        for copy in emit(half):
            copy.start()

    part_of = all_normed.at[0, pl.ds(0, 8 * HALF), :]
    pltpu.make_async_copy(part_of, part_of, c_send).wait()
    for tau in range(2):
        part_of = acts.at[0, pl.ds(0, 3)]
        pltpu.make_async_copy(part_of, part_of, x_send.at[tau]).wait()

    @pl.loop(0, ALL)
    def _(p):
        @pl.when((p < PIECES) | (p >= PIECES + 2))
        def _():
            gather.finish(p)

        @pl.when((p >= PIECES) & (p < PIECES + 2))
        def _():
            there = all_normed.at[pl.ds(0, 2)]
            pltpu.make_async_copy(there, there, send.at[p]).wait()

    @pl.loop(0, PIECES)
    def _(q):
        @pl.when(q >= 5)
        def _():
            m0(q).wait_send()

        part_of = all_normed.at[0, pl.ds(0, 7 * HALF), :]
        pltpu.make_async_copy(part_of, part_of, rs_send.at[q, 1]).wait()

    collect(2)
    for level in range(3):
        there = gains.at[level, pl.ds(0, 3)]
        pltpu.make_async_copy(there, there, g_send.at[level]).wait()
    for tau in range(2):
        swap(tau).wait()
    for copy in emit(1):
        copy.wait()


def shape(dims, dtype=BF16):
    return jax.ShapeDtypeStruct(dims, dtype)


VM = pl.BlockSpec(memory_space=pltpu.VMEM)
ANY = pl.BlockSpec(memory_space=pl.ANY)
DMA = pltpu.SemaphoreType.DMA


def block_call(features, errors, gain, w_in, w_out):
    bf16, f32 = functools.partial(pltpu.VMEM, dtype=BF16), functools.partial(
        pltpu.VMEM, dtype=F32
    )
    return pl.pallas_call(
        kernel,
        name="block",
        out_shape=(
            shape((TOK, W * PIECES)), shape((1, W * PIECES), F32),
            shape((2 * W, W)), shape((W, 2 * W)),
        ),
        in_specs=[VM, VM, VM, ANY, ANY],
        out_specs=(ANY, VM, ANY, ANY),
        scratch_shapes=[
            bf16((ALL, 16 * HALF, WIDE)),
            bf16((ALL, 16 * HALF, WIDE)),
            bf16((2, 4, GROUP, W)),
            bf16((3, W, W)),
            bf16((2, W, W)),
            bf16((3, 2, 4, 2, HALF, WIDE)),
            bf16((PIECES, 2, 4, HALF, WIDE)),
            bf16((PIECES, 2, 4, HALF, WIDE)),
            bf16((PIECES, 2, 2, HALF, W)),
            bf16((PIECES, 2, 2, HALF, WIDE)),
            bf16((PIECES, 2, HALF, WIDE)),
            bf16((PIECES, HALF, WIDE)),
            f32((2, W, W)),
            f32((2, W, W)),
            bf16((TOK, W * PIECES)),
            f32((TOK, W * PIECES)),
            f32((TOK, 128)),
            f32((TOK, W * PIECES)),
            bf16((TOK, W * PIECES)),
            bf16((6, HALF, WIDE)),
            bf16((6, HALF, WIDE)),
            f32((3, 4, 8, W)),
            *gather_scratch(ALL),
            DMA, DMA((6,)), DMA((2,)), DMA((2, 3)), DMA((2, 3)), DMA((2,)),
            DMA((PIECES, 2)), DMA((PIECES, 4)), DMA((3,)), DMA((3,)),
            DMA((2,)), DMA((2,)),
        ],
        compiler_params=pltpu.CompilerParams(
            collective_id=0, has_side_effects=True, vmem_limit_bytes=LIMIT
        ),
    )(features, errors, gain, w_in, w_out)


def emit_kernel(
    passed, gain, in_grad, out_grad,
    passed_out, gain_out, in_out, out_out,
    a, b, held_passed, held_gain, load, save,
):
    pairs = []
    for k in range(4):
        rows = pl.ds(k * 384, 384)
        pairs.append((in_grad.at[rows, :], a.at[rows, :], in_out.at[rows, :]))
        rows = pl.ds(k * 192, 192)
        pairs.append((out_grad.at[rows, :], b.at[rows, :], out_out.at[rows, :]))
    pairs.append((passed, held_passed, passed_out))
    pairs.append((gain, held_gain, gain_out))
    loads = [
        pltpu.make_async_copy(source, held, load.at[k])
        for k, (source, held, _) in enumerate(pairs)
    ]
    for copy in loads:
        copy.start()
    saves = []
    for k, (_, held, out) in enumerate(pairs):
        loads[k].wait()
        saves.append(pltpu.make_async_copy(held, out, save.at[k]))
        saves[-1].start()
    for copy in saves:
        copy.wait()


def emit_call(*results):
    return pl.pallas_call(
        emit_kernel,
        name="emit",
        out_shape=(
            shape((TOK, W * PIECES)), shape((1, W * PIECES), F32),
            shape((2 * W, W)), shape((W, 2 * W)),
        ),
        in_specs=[ANY, ANY, ANY, ANY],
        out_specs=(ANY, ANY, ANY, ANY),
        scratch_shapes=[
            pltpu.VMEM((WIDE, W), BF16), pltpu.VMEM((W, WIDE), BF16),
            pltpu.VMEM((TOK, W * PIECES), BF16), pltpu.VMEM((1, W * PIECES), F32),
            DMA((10,)), DMA((10,)),
        ],
    )(*results)


def per_device(features, delayed_error, ln_gain, w_in, w_out):
    results = block_call(features[0], delayed_error[0], ln_gain, w_in[0], w_out[0])
    passed, gain_grad, in_total, out_total = emit_call(*results)
    return passed[None], gain_grad, in_total[None], out_total[None]


def solution(mesh):
    return jax.shard_map(
        per_device,
        mesh=mesh,
        in_specs=(
            P("section", ("dp", "shard"), None),
            P("section", ("dp", "shard"), None),
            P("section", None),
            P("section", None, "shard"),
            P("section", "shard", None),
        ),
        out_specs=(
            P("section", ("dp", "shard"), None),
            P("section", None),
            P("section", "dp", "shard"),
            P("section", "shard", "dp"),
        ),
        check_vma=False,
    )
```
